768 devices in a mesh: band: 16 (over z_hi, x, core), member: 48 (over z_lo, y).
Axes of the slice: x: 4, y: 8, z: 12 (z_hi: 2, z_lo: 6; z = z_hi * 6 + z_lo), core: 2. Of those that a mesh axis runs over, the one named last changes fastest.
Arguments:
- checkpoints: float32 [48, 3, 4, 128, 512], P('member', None, None, 'band'), may hold values from -3 to 3
- ckpt_index: int32 [2], replicated, may hold values from 0 to 47, as said below
- innovations: float32 [2, 3, 4, 128, 512], P(None, None, None, 'band'), may hold values from -6 to 6
- seeds: int32 [48], P('member'), may hold values from 0 to 511
Outputs:
- adjoint: float32 [48, 3, 4, 128, 512], P('member', None, None, 'band')
The draws below stay inside these ranges and needn't reach their ends.
Inputs may be any that keep to these rules, and one draw needn't show every extreme that they name: `ckpt_index`: distinct slot indices of checkpoints, one for each interval; one of them is the last slot, 47. `seeds`: a longitude shift in cells.
All inputs are finite; a program needn't handle non-finite values.
Results may differ from the reference program's by a relative error of at most 0.0003.
Values sent between devices are 32-bit elements; how exact they have to be, the bound alone decides.
A program may use at most 32 MiB of HBM per device.

```python
import jax
import jax.numpy as jnp
from jax import lax

LEV = 4
NLON = 512
INTERVALS = 2
STEPS = 2
NROWS = 128
MEMBERS = 48
N_MEMBER = 48


def draw_ckpt_index(key, part):
    others = jax.random.permutation(jax.random.fold_in(key, 17), N_MEMBER - 1)
    chosen = jnp.concatenate([others[:INTERVALS - 1].astype(jnp.int32), jnp.full((1,), N_MEMBER - 1, jnp.int32)])
    return jax.random.permutation(jax.random.fold_in(key, 23), chosen).astype(jnp.int32)


def touch_ends(array, stream_key, smallest, largest):
    longest = array.shape.index(max(array.shape))
    spots = []
    for shift in (0, 1):
        where = [jax.random.randint(jax.random.fold_in(stream_key, axis), (), 0, length) for axis, length in enumerate(array.shape)]
        where[longest] = (where[longest] + shift) % array.shape[longest]
        spots.append(tuple(where))
    return array.at[spots[0]].set(smallest).at[spots[1]].set(largest)


def levels(rng, shape, shards, least, largest):
    gain, own = 1.0, jax.random.fold_in(rng, 6)
    for axis_at, parts in shards:
        steps = jnp.exp(jax.random.uniform(jax.random.fold_in(own, axis_at), (parts,), jnp.float32, least / len(shards), largest / len(shards)))
        gain = gain * jnp.repeat(steps, shape[axis_at] // parts).reshape([-1 if axis == axis_at else 1 for axis in range(len(shape))])
    return gain


def normal_values(stream_key, dims, scale, bound, cuts=(), kind=jnp.bfloat16):
    result = scale * jax.random.normal(stream_key, dims, jnp.float32)
    if cuts:
        result = result * levels(stream_key, dims, cuts, -0.22, 0.18)
    return jnp.clip(result, -bound, bound).astype(kind)


def setup_inputs(seed: int = 0) -> dict:
    splits = jax.random.split(jax.random.key(seed), 5)
    return {
        "checkpoints": normal_values(splits[0], (N_MEMBER, 3, LEV, NROWS, NLON), 0.5, 3.0, ((0, 48), (3, 16)), jnp.float32),
        "ckpt_index": draw_ckpt_index(jax.random.fold_in(splits[4], 71), 0),
        "innovations": normal_values(splits[2], (INTERVALS, 3, LEV, NROWS, NLON), 1.0, 6.0, ((3, 16),), jnp.float32),
        "seeds": touch_ends(jax.random.randint(splits[3], (MEMBERS,), 0, NLON), jax.random.fold_in(splits[3], 1), 0, NLON - 1).astype(jnp.int32),
    }


TIME_STEP = 0.2
VISCOSITY_BASE = 0.2


def zonal_diff(field_in):
    return 0.5 * (jnp.roll(field_in, -1, -1) - jnp.roll(field_in, 1, -1))


def advance(state):
    east_wind, north_wind, height = state[0], state[1], state[2]
    new_east = east_wind - TIME_STEP * (east_wind * zonal_diff(east_wind) + zonal_diff(height))
    new_north = north_wind - TIME_STEP * (east_wind * zonal_diff(north_wind))
    new_height = height - TIME_STEP * (east_wind * zonal_diff(height) + zonal_diff(east_wind))
    return jnp.stack([new_east, new_north, new_height])


def trajectory(initial):
    states = [initial]
    for step in range(STEPS - 1):
        states.append(advance(states[-1]))
    return states


def interior(field_in):
    return field_in[..., 1:-1, :]


def merid_diff(field_in):
    return 0.5 * (field_in[..., 2:, :] - field_in[..., :-2, :])


def laplacian(field_in):
    centre = interior(field_in)
    return field_in[..., 2:, :] + field_in[..., :-2, :] + jnp.roll(centre, -1, -1) + jnp.roll(centre, 1, -1) - 4.0 * centre


def tendency(state_ext, adjoint_ext):
    east_wind = interior(state_ext[0])
    north_wind = state_ext[1]
    layer_depth = jnp.exp(0.25 * interior(state_ext[2]))
    viscosity = VISCOSITY_BASE * (1.0 + 0.5 * jnp.tanh(state_ext[2]))
    east_part = adjoint_ext[..., 0, :, :, :]
    north_part = adjoint_ext[..., 1, :, :, :]
    height_part = adjoint_ext[..., 2, :, :, :]
    tend_east = (zonal_diff(east_wind * interior(east_part)) + merid_diff(north_wind * east_part)
                 + layer_depth * zonal_diff(interior(height_part)) + laplacian(viscosity * east_part))
    tend_north = (zonal_diff(east_wind * interior(north_part)) + merid_diff(north_wind * north_part)
                  + layer_depth * merid_diff(height_part) + laplacian(viscosity * north_part))
    tend_height = (zonal_diff(east_wind * interior(height_part)) + merid_diff(north_wind * height_part)
                   + zonal_diff(interior(east_part)) + merid_diff(north_part) + laplacian(viscosity * height_part))
    return jnp.stack([tend_east, tend_north, tend_height], axis=-4)


def shift_lon(field_in, amount):
    lon_cells = field_in.shape[-1]
    joined = jnp.concatenate([field_in, field_in], axis=-1)
    return lax.dynamic_slice_in_dim(joined, (lon_cells - amount).astype(jnp.int32), lon_cells, field_in.ndim - 1)


def pad_rows(field_in):
    return jnp.pad(field_in, [(0, 0)] * (field_in.ndim - 2) + [(1, 1), (0, 0)])


def reference(checkpoints, ckpt_index, innovations, seeds):
    paths = []
    for interval in range(INTERVALS):
        initial = lax.dynamic_index_in_dim(checkpoints, ckpt_index[interval], 0, keepdims=False)
        paths.append(trajectory(pad_rows(initial)))

    def one_member(member_seed):
        adjoint = jnp.zeros(innovations.shape[1:], jnp.float32)
        for interval in reversed(range(INTERVALS)):
            adjoint = adjoint + shift_lon(innovations[interval], member_seed)
            for step in reversed(range(STEPS)):
                adjoint = adjoint + TIME_STEP * tendency(paths[interval][step], pad_rows(adjoint))
        return adjoint

    return lax.map(one_member, seeds)
```

```python
import functools

import jax
import jax.numpy as jnp
from jax import lax
from jax.experimental import pallas as pl
from jax.experimental.pallas import tpu as pltpu
from jax.sharding import PartitionSpec as P

NY = 8
NZ = 6
NBAND = 16
LEV = 4
PLANES = 3 * LEV
HALF = PLANES // 2
ROWS = 8
LON = 512
LAST_SLOT = 47
MESH = pl.DeviceIdType.MESH


def next_lon(x):
    return pltpu.roll(x, LON - 1, 1)


def prev_lon(x):
    return pltpu.roll(x, 1, 1)


def next_row(x):
    return pltpu.roll(x, 2 * ROWS - 1, 0)


def prev_row(x):
    return pltpu.roll(x, 1, 0)


def advance(east, north, height):
    diff_east = 0.1 * (next_lon(east) - prev_lon(east))
    diff_north = 0.1 * (next_lon(north) - prev_lon(north))
    diff_height = 0.1 * (next_lon(height) - prev_lon(height))
    return (
        east - (east * diff_east + diff_height),
        north - east * diff_north,
        height - (east * diff_height + diff_east),
    )


def adjoint_step(state, adjoint, keep):
    east, north, height = state
    a, b, c = adjoint
    depth = 0.1 * jnp.exp(0.25 * height)
    visc = 0.04 + 0.02 * jnp.tanh(height)
    east, north = 0.1 * east, 0.1 * north
    c_next, c_prev = visc + east, visc - east
    r_next, r_prev = visc + north, visc - north
    middle = 1.0 - 4.0 * visc

    def spread(f, zonal=None, merid=None):
        if zonal is None:
            zonal = merid = 0.0
        return (
            middle * f
            + next_lon(c_next * f + zonal)
            + prev_lon(c_prev * f - zonal)
            + next_row(r_next * f + merid)
            + prev_row(r_prev * f - merid)
        )

    new_a = spread(a) + depth * (next_lon(c) - prev_lon(c))
    new_b = spread(b) + depth * (next_row(c) - prev_row(c))
    new_c = spread(c, 0.1 * a, 0.1 * b)
    return tuple(jnp.where(keep, f, 0.0) for f in (new_a, new_b, new_c))


def kernel(
    index_ref, seed_ref, ckpt, innov, out,
    row_in, col_in, last_in, piece, own, edge, force, force_edge,
    row_sem, col_sem, last_sem, gather_sem, place_sem, edge_sem, far_sem, force_sem, load_sem,
):
    band = lax.axis_index("band")
    member = lax.axis_index("member")
    y, z = lax.rem(member, NY), member // NY
    has_up = band < NBAND - 1
    has_down = band > 0
    up, down = {"band": band + 1}, {"band": band - 1}

    def y_peer(step):
        return lax.rem(y + step, NY)

    def z_peer(step):
        return lax.rem(z + step, NZ)

    def at_y(peer):
        return {"member": z * NY + peer}

    def at_z(peer):
        return {"member": peer * NY + y}

    def part(peer):
        planes = pl.ds(HALF * (peer // 4), HALF)
        lanes = pl.ds(pl.multiple_of(128 * lax.rem(peer, 4), 128), 128)
        return planes, slice(None), lanes

    def send(src, dst, sems, device):
        return pltpu.make_async_remote_copy(
            src_ref=src, dst_ref=dst, send_sem=sems.at[0], recv_sem=sems.at[1],
            device_id=device, device_id_type=MESH,
        )

    load = pltpu.make_async_copy(innov, force, load_sem)
    load.start()
    edge[...] = jnp.zeros_like(edge)
    force_edge[...] = jnp.zeros_like(force_edge)

    barrier = pltpu.get_barrier_semaphore()
    for step in range(1, NY):
        pl.semaphore_signal(barrier, inc=1, device_id=at_y(y_peer(step)), device_id_type=MESH)
    for step in range(1, NZ):
        pl.semaphore_signal(barrier, inc=1, device_id=at_z(z_peer(step)), device_id_type=MESH)

    @pl.when(has_up)
    def _():
        pl.semaphore_signal(barrier, inc=1, device_id=up, device_id_type=MESH)

    @pl.when(has_down)
    def _():
        pl.semaphore_signal(barrier, inc=1, device_id=down, device_id_type=MESH)

    @pl.when(jnp.logical_and(has_up, has_down))
    def _():
        pl.semaphore_wait(barrier, NY + NZ)

    @pl.when(jnp.logical_not(jnp.logical_and(has_up, has_down)))
    def _():
        pl.semaphore_wait(barrier, NY + NZ - 1)

    for step in range(1, NY):
        peer = y_peer(step)
        send(ckpt.at[part(peer)], row_in.at[y], row_sem, at_y(peer)).start()
    mine = pltpu.make_async_copy(ckpt.at[part(y)], row_in.at[y], place_sem.at[0])
    mine.start()

    def force_up(k):
        rows = (k, slice(None), slice(4, 8))
        return send(innov.at[rows], force_edge.at[rows], force_sem.at[k, 0], up)

    def force_down(k):
        rows = (k, slice(None), slice(0, 4))
        return send(innov.at[rows], force_edge.at[rows], force_sem.at[k, 1], down)

    for k in (1, 0):
        @pl.when(has_up)
        def _():
            force_up(k).start()

        @pl.when(has_down)
        def _():
            force_down(k).start()

    load.wait()
    seed = seed_ref[0]
    for k in range(2):
        for plane in range(PLANES):
            force[k, plane] = pltpu.roll(force[k, plane], seed, 1)

    mine.wait()
    send(row_in.at[pl.ds(0, NY - 1)], row_in.at[pl.ds(0, NY - 1)], row_sem, at_y(y_peer(1))).wait()

    other = jnp.where(index_ref[0] == LAST_SLOT, index_ref[1], index_ref[0])
    col_in[z] = row_in[lax.rem(other, NY)]
    for step in range(1, NZ):
        send(col_in.at[z], col_in.at[z], col_sem, at_z(z_peer(step))).start()

    @pl.when(z == NZ - 1)
    def _():
        last_in[...] = row_in[NY - 1]
        for step in range(1, NZ):
            send(last_in, last_in, last_sem, at_z(z_peer(step))).start()

    send(col_in.at[pl.ds(0, NZ - 1)], col_in.at[pl.ds(0, NZ - 1)], col_sem, at_z(z_peer(1))).wait()

    @pl.when(z == NZ - 1)
    def _():
        send(col_in.at[pl.ds(0, NZ - 1)], col_in.at[pl.ds(0, NZ - 1)], last_sem, at_z(z_peer(1))).wait_send()

    @pl.when(z < NZ - 1)
    def _():
        send(last_in, last_in, last_sem, at_z(z_peer(1))).wait_recv()

    from_other = col_in[other // NY]
    from_last = last_in[...]
    for k in (1, 0):
        piece[k] = jnp.where(index_ref[k] == LAST_SLOT, from_last, from_other)
    places = []
    for k in (1, 0):
        for step in range(1, NY):
            send(piece.at[k], own.at[(k,) + part(y)], gather_sem.at[k], at_y(y_peer(step))).start()
        places.append(pltpu.make_async_copy(piece.at[k], own.at[(k,) + part(y)], place_sem.at[1 + k]))
        places[-1].start()

    def edge_up(k):
        rows = (k, slice(None), slice(4, 8))
        return send(own.at[rows], edge.at[rows], edge_sem.at[k, 0], up)

    def edge_down(k):
        rows = (k, slice(None), slice(0, 4))
        return send(own.at[rows], edge.at[rows], edge_sem.at[k, 1], down)

    for k in (1, 0):
        @pl.when(has_up)
        def _():
            force_up(k).wait_send()
            force_down(k).wait_recv()

        @pl.when(has_down)
        def _():
            force_down(k).wait_send()
            force_up(k).wait_recv()

        for plane in range(PLANES):
            force_edge[k, plane] = pltpu.roll(force_edge[k, plane], seed, 1)

    for place, k in zip(places, (1, 0)):
        place.wait()
        send(row_in.at[pl.ds(0, NY - 1)], row_in.at[pl.ds(0, NY - 1)], gather_sem.at[k], at_y(y_peer(1))).wait()

        @pl.when(has_up)
        def _():
            edge_up(k).start()

        @pl.when(has_down)
        def _():
            edge_down(k).start()

    row = lax.broadcasted_iota(jnp.int32, (2 * ROWS, LON), 0)
    outside = jnp.logical_or(
        jnp.logical_and(band == NBAND - 1, jnp.logical_and(row >= 8, row < 12)),
        jnp.logical_and(band == 0, row >= 12),
    )
    keep = jnp.logical_not(outside)

    adjoint = [None] * LEV
    for k in (1, 0):
        @pl.when(has_up)
        def _():
            edge_up(k).wait_send()
            edge_down(k).wait_recv()

        @pl.when(has_down)
        def _():
            edge_down(k).wait_send()
            edge_up(k).wait_recv()

        for lev in range(LEV):
            def both(inner, outer):
                return tuple(
                    jnp.concatenate([inner[k, comp * LEV + lev], outer[k, comp * LEV + lev]], axis=0)
                    for comp in range(3)
                )

            forcing = both(force, force_edge)
            if adjoint[lev] is None:
                field = forcing
            else:
                field = tuple(f + g for f, g in zip(adjoint[lev], forcing))
            first = both(own, edge)
            field = adjoint_step(advance(*first), field, keep)
            field = adjoint_step(first, field, keep)
            if k == 1:
                adjoint[lev] = field
            else:
                for comp in range(3):
                    out[comp * LEV + lev] = field[comp][:ROWS]


def on_device(checkpoints, ckpt_index, innovations, seeds):
    slot = checkpoints.reshape(PLANES, ROWS, LON)
    current = innovations.reshape(2, PLANES, ROWS, LON)
    any_space = pl.BlockSpec(memory_space=pl.ANY)
    smem = pl.BlockSpec(memory_space=pltpu.SMEM)
    field = (2, PLANES, ROWS, LON)
    dma = pltpu.SemaphoreType.DMA
    result = pl.pallas_call(
        kernel,
        out_shape=jax.ShapeDtypeStruct((PLANES, ROWS, LON), jnp.float32),
        in_specs=[smem, smem, any_space, any_space],
        out_specs=pl.BlockSpec(memory_space=pltpu.VMEM),
        scratch_shapes=[
            pltpu.VMEM((NY, HALF, ROWS, 128), jnp.float32),
            pltpu.VMEM((NZ, HALF, ROWS, 128), jnp.float32),
            pltpu.VMEM((HALF, ROWS, 128), jnp.float32),
            pltpu.VMEM((2, HALF, ROWS, 128), jnp.float32),
            pltpu.VMEM(field, jnp.float32),
            pltpu.VMEM(field, jnp.float32),
            pltpu.VMEM(field, jnp.float32),
            pltpu.VMEM(field, jnp.float32),
            dma((2,)),
            dma((2,)),
            dma((2,)),
            dma((2, 2)),
            dma((3,)),
            dma((2, 2, 2)),
            dma((2,)),
            dma((2, 2, 2)),
            dma,
        ],
        compiler_params=pltpu.CompilerParams(
            collective_id=0, has_side_effects=True, vmem_limit_bytes=32 * 2**20
        ),
        name="ensemble_adjoint",
    )(ckpt_index, seeds, slot, current)
    return result.reshape(1, 3, LEV, ROWS, LON)


def solution(mesh):
    return jax.shard_map(
        on_device,
        mesh=mesh,
        in_specs=(
            P("member", None, None, "band", None),
            P(),
            P(None, None, None, "band", None),
            P("member"),
        ),
        out_specs=P("member", None, None, "band", None),
        check_vma=False,
    )
```

```python
import jax
import jax.numpy as jnp
from jax import lax
from jax.experimental import pallas as pl
from jax.experimental.pallas import tpu as pltpu
from jax.sharding import PartitionSpec as P

NY = 8
NZ = 6
NBAND = 16
LOW_FAR, HIGH_FAR = NBAND // 2 - 1, NBAND // 2
LEV = 4
PLANES = 3 * LEV
HALF = PLANES // 2
ROWS = 8
LON = 512
LAST_SLOT = NY * NZ - 1
EDGE = {1: 4, 0: 2}
MESH = pl.DeviceIdType.MESH


def next_lon(x):
    return pltpu.roll(x, LON - 1, 1)


def prev_lon(x):
    return pltpu.roll(x, 1, 1)


def next_row(x):
    return pltpu.roll(x, 2 * ROWS - 1, 0)


def prev_row(x):
    return pltpu.roll(x, 1, 0)


def advance(east, north, height):
    diff_east = 0.1 * (next_lon(east) - prev_lon(east))
    diff_north = 0.1 * (next_lon(north) - prev_lon(north))
    diff_height = 0.1 * (next_lon(height) - prev_lon(height))
    return (
        east - (east * diff_east + diff_height),
        north - east * diff_north,
        height - (east * diff_height + diff_east),
    )


def adjoint_step(state, adjoint, keep):
    east, north, height = state
    a, b, c = adjoint
    depth = 0.1 * jnp.exp(0.25 * height)
    visc = 0.04 + 0.02 * jnp.tanh(height)
    east, north = 0.1 * east, 0.1 * north
    c_next, c_prev = visc + east, visc - east
    r_next, r_prev = visc + north, visc - north
    middle = 1.0 - 4.0 * visc

    def spread(f, zonal=None, merid=None):
        if zonal is None:
            zonal = merid = 0.0
        return (
            middle * f
            + next_lon(c_next * f + zonal)
            + prev_lon(c_prev * f - zonal)
            + next_row(r_next * f + merid)
            + prev_row(r_prev * f - merid)
        )

    new_a = spread(a) + depth * (next_lon(c) - prev_lon(c))
    new_b = spread(b) + depth * (next_row(c) - prev_row(c))
    new_c = spread(c, 0.1 * a, 0.1 * b)
    return tuple(jnp.where(keep, f, 0.0) for f in (new_a, new_b, new_c))


def kernel(
    index_hbm, seed_ref, ckpt, innov, out,
    index_ref,
    p_row, p_col, p_last, p_mine, p_edge,
    q_col, q_row, q_last, q_mine, q_edge,
    own, edge, force, force_edge,
    p_sem, q_sem, gather_sem, far_sem, spread_sem, edge_sem, force_sem, local_sem,
):
    band = lax.axis_index("band")
    member = lax.axis_index("member")
    y, z = lax.rem(member, NY), member // NY
    is_low, is_high = band == LOW_FAR, band == HIGH_FAR
    is_far = jnp.logical_or(is_low, is_high)
    near_up = jnp.logical_and(band < NBAND - 1, jnp.logical_not(is_low))
    near_down = jnp.logical_and(band > 0, jnp.logical_not(is_high))
    at_end = jnp.logical_or(band == 0, band == NBAND - 1)
    up, down = {"band": band + 1}, {"band": band - 1}
    far = {"band": NBAND - 1 - band, "member": (NZ - 1 - z) * NY + y}

    y_peers = [lax.rem(y + step, NY) for step in range(1, NY)]
    z_peers = [lax.rem(z + step, NZ) for step in range(1, NZ)]

    def at_y(peer):
        return {"member": z * NY + peer}

    def at_z(peer):
        return {"member": peer * NY + y}

    def low_rows(k):
        return slice(0, EDGE[k])

    def high_rows(k):
        return slice(ROWS - EDGE[k], ROWS)

    def p_part(peer, rows=slice(None)):
        planes = pl.ds((HALF // 2) * (peer // 4), HALF // 2)
        return planes, rows, pl.ds(pl.multiple_of(128 * lax.rem(peer, 4), 128), 128)

    def q_part(peer, rows=slice(None)):
        return HALF + peer, rows

    def send(src, dst, sems, device):
        return pltpu.make_async_remote_copy(
            src_ref=src, dst_ref=dst, send_sem=sems.at[0], recv_sem=sems.at[1],
            device_id=device, device_id_type=MESH,
        )

    def drain(ref, sems):
        return send(ref, ref, sems, at_y(y_peers[0]))

    def copy(src, dst, slot):
        return pltpu.make_async_copy(src, dst, local_sem.at[slot])

    load_index = copy(index_hbm, index_ref, 11)
    load = copy(innov, force, 0)
    load_index.start()
    load.start()
    edge[...] = jnp.zeros_like(edge)
    force_edge[...] = jnp.zeros_like(force_edge)

    barrier = pltpu.get_barrier_semaphore()

    def greet(device):
        pl.semaphore_signal(barrier, inc=1, device_id=device, device_id_type=MESH)

    for peer in z_peers:
        greet(at_z(peer))
    for peer in y_peers:
        greet(at_y(peer))
    pl.when(near_up)(lambda: greet(up))
    pl.when(near_down)(lambda: greet(down))
    pl.when(is_far)(lambda: greet(far))
    pl.when(at_end)(lambda: pl.semaphore_wait(barrier, NY + NZ - 1))
    pl.when(jnp.logical_not(at_end))(lambda: pl.semaphore_wait(barrier, NY + NZ))

    for peer in z_peers:
        send(ckpt.at[q_part(peer)], q_col.at[z], q_sem.at[0], at_z(peer)).start()
    for peer in y_peers:
        send(ckpt.at[p_part(peer)], p_row.at[y], p_sem.at[0], at_y(peer)).start()
    p_keep = copy(ckpt.at[p_part(y)], p_row.at[y], 1)
    q_keep = copy(ckpt.at[q_part(z)], q_col.at[z], 2)
    p_keep.start()
    q_keep.start()

    def edge_up(src, dst, sems, k, device):
        rows = (k, slice(None), high_rows(k))
        return send(src(k, high_rows(k)), dst.at[rows], sems.at[k, 0], device)

    def edge_down(src, dst, sems, k, device):
        rows = (k, slice(None), low_rows(k))
        return send(src(k, low_rows(k)), dst.at[rows], sems.at[k, 1], device)

    def start_edges(src, dst, sems, k, with_far):
        pl.when(near_up)(lambda: edge_up(src, dst, sems, k, up).start())
        pl.when(near_down)(lambda: edge_down(src, dst, sems, k, down).start())
        if with_far:
            pl.when(is_low)(lambda: edge_up(src, dst, sems, k, far).start())
            pl.when(is_high)(lambda: edge_down(src, dst, sems, k, far).start())

    def finish_edges(src, dst, sems, k, with_far):
        def upper():
            edge_up(src, dst, sems, k, up).wait_send()
            edge_down(src, dst, sems, k, up).wait_recv()

        def lower():
            edge_down(src, dst, sems, k, down).wait_send()
            edge_up(src, dst, sems, k, down).wait_recv()

        pl.when(near_up)(upper)
        pl.when(near_down)(lower)
        if with_far:
            pl.when(is_low)(upper)
            pl.when(is_high)(lower)

    def innov_rows(k, rows):
        return innov.at[k, :, rows]

    def own_rows(k, rows):
        return own.at[k, :, rows]

    for k in (1, 0):
        start_edges(innov_rows, force_edge, force_sem, k, True)

    load_index.wait()
    seed = seed_ref[0]
    index = [index_ref[0], index_ref[1]]
    other = jnp.where(index[0] == LAST_SLOT, index[1], index[0])
    load.wait()
    for k in range(2):
        for plane in range(PLANES):
            force[k, plane] = pltpu.roll(force[k, plane], seed, 1)

    p_keep.wait()
    drain(p_row.at[pl.ds(0, NY - 1)], p_sem.at[0]).wait()
    p_col[z] = p_row[lax.rem(other, NY)]
    for peer in z_peers:
        send(p_col.at[z], p_col.at[z], p_sem.at[1], at_z(peer)).start()

    @pl.when(z == NZ - 1)
    def _():
        p_last[...] = p_row[NY - 1]
        for peer in z_peers:
            send(p_last, p_last, p_sem.at[2], at_z(peer)).start()

    q_keep.wait()
    drain(q_col.at[pl.ds(0, NZ - 1)], q_sem.at[0]).wait()
    q_row[y] = q_col[other // NY]
    for peer in y_peers:
        send(q_row.at[y], q_row.at[y], q_sem.at[1], at_y(peer)).start()

    @pl.when(y == NY - 1)
    def _():
        q_last[...] = q_col[NZ - 1]
        for peer in y_peers:
            send(q_last, q_last, q_sem.at[2], at_y(peer)).start()

    drain(p_col.at[pl.ds(0, NZ - 1)], p_sem.at[1]).wait()
    pl.when(z == NZ - 1)(lambda: drain(p_col.at[pl.ds(0, NZ - 1)], p_sem.at[2]).wait_send())
    pl.when(z < NZ - 1)(lambda: drain(p_last, p_sem.at[2]).wait_recv())
    from_other, from_last = p_col[other // NY], p_last[...]
    for k in (1, 0):
        p_mine[k] = jnp.where(index[k] == LAST_SLOT, from_last, from_other)
    keeps = []
    for k in (1, 0):
        for peer in y_peers:
            send(p_mine.at[k], own.at[(k,) + p_part(y)], gather_sem.at[k, 0], at_y(peer)).start()
        keeps.append(copy(p_mine.at[k], own.at[(k,) + p_part(y)], 3 + k))
        keeps[-1].start()

    def far_rows(mine, landing, sems, job):
        for k in (1, 0):
            def low():
                rows = (k,) + (slice(None),) * (len(mine.shape) - 3)
                getattr(send(mine.at[rows + (high_rows(k),)], landing.at[rows + (high_rows(k),)], sems.at[k], far), job)()

            def high():
                rows = (k,) + (slice(None),) * (len(mine.shape) - 3)
                getattr(send(mine.at[rows + (low_rows(k),)], landing.at[rows + (low_rows(k),)], sems.at[k], far), job)()

            if job == "wait_recv":
                low, high = high, low
            pl.when(is_low)(low)
            pl.when(is_high)(high)

    far_rows(p_mine, p_edge, far_sem.at[0], "start")

    drain(q_row.at[pl.ds(0, NY - 1)], q_sem.at[1]).wait()
    pl.when(y == NY - 1)(lambda: drain(q_row.at[pl.ds(0, NY - 1)], q_sem.at[2]).wait_send())
    pl.when(y < NY - 1)(lambda: drain(q_last, q_sem.at[2]).wait_recv())
    from_other, from_last = q_row[lax.rem(other, NY)], q_last[...]
    for k in (1, 0):
        q_mine[k] = jnp.where(index[k] == LAST_SLOT, from_last, from_other)
    for k in (1, 0):
        for peer in z_peers:
            send(q_mine.at[k], own.at[(k,) + q_part(z)], gather_sem.at[k, 1], at_z(peer)).start()
        keeps.append(copy(q_mine.at[k], own.at[(k,) + q_part(z)], 5 + k))
        keeps[-1].start()
    far_rows(q_mine, q_edge, far_sem.at[1], "start")

    far_rows(p_mine, p_edge, far_sem.at[0], "wait_recv")
    for k in (1, 0):
        def pass_p(rows):
            for peer in y_peers:
                send(p_edge.at[k, :, rows], edge.at[(k,) + p_part(y, rows)], spread_sem.at[k, 0], at_y(peer)).start()
            copy(p_edge.at[k, :, rows], edge.at[(k,) + p_part(y, rows)], 7 + k).start()

        pl.when(is_low)(lambda: pass_p(low_rows(k)))
        pl.when(is_high)(lambda: pass_p(high_rows(k)))
    far_rows(q_mine, q_edge, far_sem.at[1], "wait_recv")
    for k in (1, 0):
        def pass_q(rows):
            for peer in z_peers:
                send(q_edge.at[k, rows], edge.at[(k,) + q_part(NZ - 1 - z, rows)], spread_sem.at[k, 1], at_z(peer)).start()
            copy(q_edge.at[k, rows], edge.at[(k,) + q_part(NZ - 1 - z, rows)], 9 + k).start()

        pl.when(is_low)(lambda: pass_q(low_rows(k)))
        pl.when(is_high)(lambda: pass_q(high_rows(k)))

    for k in (1, 0):
        finish_edges(innov_rows, force_edge, force_sem, k, True)
        for plane in range(PLANES):
            force_edge[k, plane] = pltpu.roll(force_edge[k, plane], seed, 1)

    for job in keeps:
        job.wait()
    for k in (1, 0):
        drain(p_row.at[pl.ds(0, NY - 1)], gather_sem.at[k, 0]).wait()
        drain(q_col.at[pl.ds(0, NZ - 1)], gather_sem.at[k, 1]).wait()
        start_edges(own_rows, edge, edge_sem, k, False)

    row = lax.broadcasted_iota(jnp.int32, (2 * ROWS, LON), 0)
    outside = jnp.logical_or(
        jnp.logical_and(band == NBAND - 1, jnp.logical_and(row >= 8, row < 12)),
        jnp.logical_and(band == 0, row >= 12),
    )
    keep = jnp.logical_not(outside)

    adjoint = [None] * LEV
    for k in (1, 0):
        finish_edges(own_rows, edge, edge_sem, k, False)

        @pl.when(is_far)
        def _():
            rows = low_rows(k)
            drain(p_row.at[pl.ds(0, NY - 1), :, rows], spread_sem.at[k, 0]).wait()
            drain(q_col.at[pl.ds(0, NZ - 1), rows], spread_sem.at[k, 1]).wait()
            copy(p_edge.at[k, :, rows], p_edge.at[k, :, rows], 7 + k).wait()
            copy(q_edge.at[k, rows], q_edge.at[k, rows], 9 + k).wait()

        for lev in range(LEV):
            def both(inner, outer):
                return tuple(
                    jnp.concatenate([inner[k, comp * LEV + lev], outer[k, comp * LEV + lev]], axis=0)
                    for comp in range(3)
                )

            forcing = both(force, force_edge)
            if adjoint[lev] is None:
                field = forcing
            else:
                field = tuple(f + g for f, g in zip(adjoint[lev], forcing))
            first = both(own, edge)
            field = adjoint_step(advance(*first), field, keep)
            field = adjoint_step(first, field, keep)
            if k == 1:
                adjoint[lev] = field
            else:
                for comp in range(3):
                    out[comp * LEV + lev] = field[comp][:ROWS]

    far_rows(p_mine, p_edge, far_sem.at[0], "wait_send")
    far_rows(q_mine, q_edge, far_sem.at[1], "wait_send")


def on_device(checkpoints, ckpt_index, innovations, seeds):
    slot = checkpoints.reshape(PLANES, ROWS, LON)
    current = innovations.reshape(2, PLANES, ROWS, LON)
    hbm = pl.BlockSpec(memory_space=pltpu.HBM)
    slot, current, ckpt_index = (
        pltpu.with_memory_space_constraint(operand, pltpu.HBM) for operand in (slot, current, ckpt_index)
    )
    field = (2, PLANES, ROWS, LON)
    dma = pltpu.SemaphoreType.DMA

    def vmem(*shape):
        return pltpu.VMEM(shape, jnp.float32)

    result = pl.pallas_call(
        kernel,
        out_shape=jax.ShapeDtypeStruct((PLANES, ROWS, LON), jnp.float32),
        in_specs=[hbm, pl.BlockSpec(memory_space=pltpu.SMEM), hbm, hbm],
        out_specs=pl.BlockSpec(memory_space=pltpu.VMEM),
        scratch_shapes=[
            pltpu.SMEM((2,), jnp.int32),
            vmem(NY, HALF // 2, ROWS, 128),
            vmem(NZ, HALF // 2, ROWS, 128),
            vmem(HALF // 2, ROWS, 128),
            vmem(2, HALF // 2, ROWS, 128),
            vmem(2, HALF // 2, ROWS, 128),
            vmem(NZ, ROWS, LON),
            vmem(NY, ROWS, LON),
            vmem(ROWS, LON),
            vmem(2, ROWS, LON),
            vmem(2, ROWS, LON),
            vmem(*field),
            vmem(*field),
            vmem(*field),
            vmem(*field),
            dma((3, 2)),
            dma((3, 2)),
            dma((2, 2, 2)),
            dma((2, 2, 2)),
            dma((2, 2, 2)),
            dma((2, 2, 2)),
            dma((2, 2, 2)),
            dma((12,)),
        ],
        compiler_params=pltpu.CompilerParams(
            collective_id=0, has_side_effects=True, vmem_limit_bytes=32 * 2**20
        ),
        name="ensemble_adjoint",
    )(ckpt_index, seeds, slot, current)
    return result.reshape(1, 3, LEV, ROWS, LON)


def solution(mesh):
    return jax.shard_map(
        on_device,
        mesh=mesh,
        in_specs=(
            P("member", None, None, "band", None),
            P(),
            P(None, None, None, "band", None),
            P("member"),
        ),
        out_specs=P("member", None, None, "band", None),
        check_vma=False,
    )
```

```python
import jax
import jax.numpy as jnp
from jax import lax
from jax.experimental import pallas as pl
from jax.experimental.pallas import tpu as pltpu
from jax.sharding import PartitionSpec as P

NY = 8
NZ = 6
NBAND = 16
LOW_FAR, HIGH_FAR = NBAND // 2 - 1, NBAND // 2
LEV = 4
PLANES = 3 * LEV
HALF = PLANES // 2
ROWS = 8
LON = 512
LAST_SLOT = NY * NZ - 1
EDGE = {1: 4, 0: 2}
MESH = pl.DeviceIdType.MESH


def next_lon(x):
    return pltpu.roll(x, LON - 1, 1)


def prev_lon(x):
    return pltpu.roll(x, 1, 1)


def next_row(x):
    return pltpu.roll(x, 2 * ROWS - 1, 0)


def prev_row(x):
    return pltpu.roll(x, 1, 0)


def advance(east, north, height):
    diff_east = 0.1 * (next_lon(east) - prev_lon(east))
    diff_north = 0.1 * (next_lon(north) - prev_lon(north))
    diff_height = 0.1 * (next_lon(height) - prev_lon(height))
    return (
        east - (east * diff_east + diff_height),
        north - east * diff_north,
        height - (east * diff_height + diff_east),
    )


def adjoint_step(state, adjoint, keep):
    east, north, height = state
    a, b, c = adjoint
    depth = 0.1 * jnp.exp(0.25 * height)
    visc = 0.04 + 0.02 * jnp.tanh(height)
    east, north = 0.1 * east, 0.1 * north
    c_next, c_prev = visc + east, visc - east
    r_next, r_prev = visc + north, visc - north
    middle = 1.0 - 4.0 * visc

    def spread(f, zonal=None, merid=None):
        if zonal is None:
            zonal = merid = 0.0
        return (
            middle * f
            + next_lon(c_next * f + zonal)
            + prev_lon(c_prev * f - zonal)
            + next_row(r_next * f + merid)
            + prev_row(r_prev * f - merid)
        )

    new_a = spread(a) + depth * (next_lon(c) - prev_lon(c))
    new_b = spread(b) + depth * (next_row(c) - prev_row(c))
    new_c = spread(c, 0.1 * a, 0.1 * b)
    return tuple(jnp.where(keep, f, 0.0) for f in (new_a, new_b, new_c))


def kernel(
    index_hbm, seed_ref, ckpt, innov, out,
    index_ref, slot,
    p_row, p_col, p_last, p_mine, p_edge,
    q_col, q_row, q_last, q_mine, q_edge,
    h_slot, h_row, h_col, h_last, h_mine,
    own, edge, force, force_edge,
    p_sem, q_sem, h_sem, gather_sem, cross_sem, spread_sem, h_gather_sem, edge_sem, force_sem, local_sem,
):
    band = lax.axis_index("band")
    member = lax.axis_index("member")
    y, z = lax.rem(member, NY), member // NY
    odd = lax.rem(band, 2) == 1
    even = jnp.logical_not(odd)
    is_low, is_high = band == LOW_FAR, band == HIGH_FAR
    is_far = jnp.logical_or(is_low, is_high)
    near_up = jnp.logical_and(band < NBAND - 1, jnp.logical_not(is_low))
    near_down = jnp.logical_and(band > 0, jnp.logical_not(is_high))
    cross_up, cross_down = jnp.logical_and(odd, near_up), jnp.logical_and(even, near_down)
    at_end = jnp.logical_or(band == 0, band == NBAND - 1)
    up, down = {"band": band + 1}, {"band": band - 1}
    far = {"band": NBAND - 1 - band, "member": (NZ - 1 - z) * NY + y}

    y_peers = [lax.rem(y + step, NY) for step in range(1, NY)]
    z_peers = [lax.rem(z + step, NZ) for step in range(1, NZ)]

    def at_y(peer):
        return {"member": z * NY + peer}

    def at_z(peer):
        return {"member": peer * NY + y}

    def low_rows(k):
        return slice(0, EDGE[k])

    def high_rows(k):
        return slice(ROWS - EDGE[k], ROWS)

    def p_part(peer, rows=slice(None)):
        planes = pl.ds((HALF // 2) * (peer // 4), HALF // 2)
        return planes, rows, pl.ds(pl.multiple_of(128 * lax.rem(peer, 4), 128), 128)

    def q_part(peer, rows=slice(None)):
        return HALF + peer, rows

    def h_part(peer, rows):
        planes = pl.ds(HALF * (peer // 4), HALF)
        return planes, rows, pl.ds(pl.multiple_of(128 * lax.rem(peer, 4), 128), 128)

    def send(src, dst, sems, device):
        return pltpu.make_async_remote_copy(
            src_ref=src, dst_ref=dst, send_sem=sems.at[0], recv_sem=sems.at[1],
            device_id=device, device_id_type=MESH,
        )

    def drain(ref, sems):
        return send(ref, ref, sems, at_y(y_peers[0]))

    def copy(src, dst, number):
        return pltpu.make_async_copy(src, dst, local_sem.at[number])

    def both_sides(at_odd, at_even, job):
        pl.when(at_odd)(lambda: job(high_rows, low_rows, up))
        pl.when(at_even)(lambda: job(low_rows, high_rows, down))

    barrier = pltpu.get_barrier_semaphore()

    def greet(device):
        pl.semaphore_signal(barrier, inc=1, device_id=device, device_id_type=MESH)

    for peer in z_peers:
        greet(at_z(peer))
    for peer in y_peers:
        greet(at_y(peer))
    pl.when(near_up)(lambda: greet(up))
    pl.when(near_down)(lambda: greet(down))
    pl.when(is_far)(lambda: greet(far))

    load_slot = copy(ckpt, slot, 0)
    load_index = copy(index_hbm, index_ref, 1)
    load_force = copy(innov, force, 2)
    load_slot.start()
    load_index.start()
    load_force.start()
    load_slot.wait()
    p_row[y] = slot[p_part(y)]
    q_col[z] = slot[q_part(z)]

    pl.when(at_end)(lambda: pl.semaphore_wait(barrier, NY + NZ - 1))
    pl.when(jnp.logical_not(at_end))(lambda: pl.semaphore_wait(barrier, NY + NZ))

    for peer in z_peers:
        send(slot.at[q_part(peer)], q_col.at[z], q_sem.at[0], at_z(peer)).start()
    for peer in y_peers:
        send(slot.at[p_part(peer)], p_row.at[y], p_sem.at[0], at_y(peer)).start()

    def far_slot(sent, got, device):
        send(slot.at[:, sent(1)], h_slot.at[:, sent(1)], h_sem.at[0], far).start()

    both_sides(is_low, is_high, far_slot)

    def edge_up(src, dst, sems, k, device):
        rows = (k, slice(None), high_rows(k))
        return send(src.at[rows], dst.at[rows], sems.at[k, 0], device)

    def edge_down(src, dst, sems, k, device):
        rows = (k, slice(None), low_rows(k))
        return send(src.at[rows], dst.at[rows], sems.at[k, 1], device)

    def start_edges(src, dst, sems, k, upward, downward):
        pl.when(upward)(lambda: edge_up(src, dst, sems, k, up).start())
        pl.when(downward)(lambda: edge_down(src, dst, sems, k, down).start())

    def finish_edges(src, dst, sems, k, upward, downward):
        def upper():
            edge_up(src, dst, sems, k, up).wait_send()
            edge_down(src, dst, sems, k, up).wait_recv()

        def lower():
            edge_down(src, dst, sems, k, down).wait_send()
            edge_up(src, dst, sems, k, down).wait_recv()

        pl.when(upward)(upper)
        pl.when(downward)(lower)

    for k in (1, 0):
        start_edges(innov, force_edge, force_sem, k, near_up, near_down)
        pl.when(is_low)(lambda: edge_up(innov, force_edge, force_sem, k, far).start())
        pl.when(is_high)(lambda: edge_down(innov, force_edge, force_sem, k, far).start())

    load_index.wait()
    seed = seed_ref[0]
    index = [index_ref[0], index_ref[1]]
    other = jnp.where(index[0] == LAST_SLOT, index[1], index[0])
    other_y, other_z = lax.rem(other, NY), other // NY
    load_force.wait()
    for k in range(2):
        for plane in range(PLANES):
            force[k, plane] = pltpu.roll(force[k, plane], seed, 1)

    drain(p_row.at[pl.ds(0, NY - 1)], p_sem.at[0]).wait()
    p_col[z] = p_row[other_y]
    for peer in z_peers:
        send(p_col.at[z], p_col.at[z], p_sem.at[1], at_z(peer)).start()

    @pl.when(z == NZ - 1)
    def _():
        p_last[...] = p_row[NY - 1]
        for peer in z_peers:
            send(p_last, p_last, p_sem.at[2], at_z(peer)).start()

    drain(q_col.at[pl.ds(0, NZ - 1)], q_sem.at[0]).wait()
    q_row[y] = q_col[other_z]
    for peer in y_peers:
        send(q_row.at[y], q_row.at[y], q_sem.at[1], at_y(peer)).start()

    @pl.when(y == NY - 1)
    def _():
        q_last[...] = q_col[NZ - 1]
        for peer in y_peers:
            send(q_last, q_last, q_sem.at[2], at_y(peer)).start()

    def far_row(sent, got, device):
        send(slot.at[:, sent(1)], h_slot.at[:, sent(1)], h_sem.at[0], far).wait_send()
        send(h_slot.at[:, got(1)], h_slot.at[:, got(1)], h_sem.at[0], far).wait_recv()
        for peer in y_peers:
            send(h_slot.at[h_part(peer, got(1))], h_row.at[y, :, got(1)], h_sem.at[1], at_y(peer)).start()
        h_row[y, :, got(1)] = h_slot[h_part(y, got(1))]

    both_sides(is_low, is_high, far_row)

    drain(p_col.at[pl.ds(0, NZ - 1)], p_sem.at[1]).wait()
    pl.when(z == NZ - 1)(lambda: drain(p_col.at[pl.ds(0, NZ - 1)], p_sem.at[2]).wait_send())
    pl.when(z < NZ - 1)(lambda: drain(p_last, p_sem.at[2]).wait_recv())
    from_other, from_last = p_col[other_z], p_last[...]
    for k in (1, 0):
        p_mine[k] = jnp.where(index[k] == LAST_SLOT, from_last, from_other)

    def cross_p(sent, got, device):
        send(p_mine.at[0, :, sent(0)], p_edge.at[:, sent(0)], cross_sem.at[0], device).start()

    both_sides(cross_up, cross_down, cross_p)
    for k in (1, 0):
        for peer in y_peers:
            send(p_mine.at[k], own.at[(k,) + p_part(y)], gather_sem.at[k, 0], at_y(peer)).start()
        own[(k,) + p_part(y)] = p_mine[k]

    def far_col(sent, got, device):
        drain(h_row.at[pl.ds(0, NY - 1), :, got(1)], h_sem.at[1]).wait()
        h_col[z, :, got(1)] = h_row[other_y, :, got(1)]
        for peer in z_peers:
            send(h_col.at[z, :, got(1)], h_col.at[z, :, got(1)], h_sem.at[2], at_z(peer)).start()

        @pl.when(z == 0)
        def _():
            h_last[:, got(1)] = h_row[NY - 1, :, got(1)]
            for peer in z_peers:
                send(h_last.at[:, got(1)], h_last.at[:, got(1)], h_sem.at[3], at_z(peer)).start()

    both_sides(is_low, is_high, far_col)

    drain(q_row.at[pl.ds(0, NY - 1)], q_sem.at[1]).wait()
    pl.when(y == NY - 1)(lambda: drain(q_row.at[pl.ds(0, NY - 1)], q_sem.at[2]).wait_send())
    pl.when(y < NY - 1)(lambda: drain(q_last, q_sem.at[2]).wait_recv())
    from_other, from_last = q_row[other_y], q_last[...]
    for k in (1, 0):
        q_mine[k] = jnp.where(index[k] == LAST_SLOT, from_last, from_other)

    def cross_q(sent, got, device):
        send(q_mine.at[0, sent(0)], q_edge.at[sent(0)], cross_sem.at[1], device).start()

    both_sides(cross_up, cross_down, cross_q)
    for k in (1, 0):
        for peer in z_peers:
            send(q_mine.at[k], own.at[(k,) + q_part(z)], gather_sem.at[k, 1], at_z(peer)).start()
        own[(k,) + q_part(z)] = q_mine[k]

    def spread_p(sent, got, device):
        drain(p_edge.at[:, got(0)], cross_sem.at[0]).wait()
        for peer in y_peers:
            send(p_edge.at[:, got(0)], edge.at[(0,) + p_part(y, got(0))], spread_sem.at[0], at_y(peer)).start()
        edge[(0,) + p_part(y, got(0))] = p_edge[:, got(0)]

    def spread_q(sent, got, device):
        drain(q_edge.at[got(0)], cross_sem.at[1]).wait()
        for peer in z_peers:
            send(q_edge.at[got(0)], edge.at[(0,) + q_part(z, got(0))], spread_sem.at[1], at_z(peer)).start()
        edge[(0,) + q_part(z, got(0))] = q_edge[got(0)]

    both_sides(cross_up, cross_down, spread_p)
    both_sides(cross_up, cross_down, spread_q)

    def far_gather(sent, got, device):
        drain(h_col.at[pl.ds(0, NZ - 1), :, got(1)], h_sem.at[2]).wait()
        pl.when(z == 0)(lambda: drain(h_col.at[pl.ds(0, NZ - 1), :, got(1)], h_sem.at[3]).wait_send())
        pl.when(z > 0)(lambda: drain(h_last.at[:, got(1)], h_sem.at[3]).wait_recv())
        from_other, from_last = h_col[NZ - 1 - other_z, :, got(1)], h_last[:, got(1)]
        for k in (1, 0):
            h_mine[k, :, got(1)] = jnp.where(index[k] == LAST_SLOT, from_last, from_other)
            for peer in y_peers:
                send(
                    h_mine.at[k, :, got(k)], edge.at[(k,) + h_part(y, got(k))], h_gather_sem.at[k], at_y(peer)
                ).start()
            edge[(k,) + h_part(y, got(k))] = h_mine[k, :, got(k)]

    both_sides(is_low, is_high, far_gather)

    for k in (1, 0):
        finish_edges(innov, force_edge, force_sem, k, band < NBAND - 1, band > 0)
        for plane in range(PLANES):
            force_edge[k, plane] = pltpu.roll(force_edge[k, plane], seed, 1)

    needs_up, needs_down = {1: near_up, 0: even}, {1: near_down, 0: odd}
    for k in (1, 0):
        drain(p_row.at[pl.ds(0, NY - 1)], gather_sem.at[k, 0]).wait()
        drain(q_col.at[pl.ds(0, NZ - 1)], gather_sem.at[k, 1]).wait()
        start_edges(own, edge, edge_sem, k, needs_up[k], needs_down[k])

    row = lax.broadcasted_iota(jnp.int32, (ROWS, LON), 0)
    inside = jnp.logical_not(
        jnp.logical_or(
            jnp.logical_and(band == NBAND - 1, row < ROWS // 2),
            jnp.logical_and(band == 0, row >= ROWS // 2),
        )
    )
    keep = jnp.logical_or(
        lax.broadcasted_iota(jnp.int32, (2 * ROWS, LON), 0) < ROWS,
        jnp.concatenate([inside, inside], axis=0),
    )

    adjoint = [None] * LEV
    for k in (1, 0):
        finish_edges(own, edge, edge_sem, k, needs_up[k], needs_down[k])
        if k == 0:
            def spread_done(sent, got, device):
                drain(p_row.at[pl.ds(0, NY - 1), :, got(0)], spread_sem.at[0]).wait()
                drain(q_col.at[pl.ds(0, NZ - 1), got(0)], spread_sem.at[1]).wait()

            both_sides(cross_up, cross_down, spread_done)

        def far_done(sent, got, device):
            drain(h_row.at[pl.ds(0, NY - 1), :, got(k)], h_gather_sem.at[k]).wait()

        both_sides(is_low, is_high, far_done)

        for lev in range(LEV):
            def both(inner, outer):
                return tuple(
                    jnp.concatenate(
                        [inner[k, comp * LEV + lev], jnp.where(inside, outer[k, comp * LEV + lev], 0.0)], axis=0
                    )
                    for comp in range(3)
                )

            forcing = both(force, force_edge)
            if adjoint[lev] is None:
                field = forcing
            else:
                field = tuple(f + g for f, g in zip(adjoint[lev], forcing))
            first = both(own, edge)
            field = adjoint_step(advance(*first), field, keep)
            field = adjoint_step(first, field, keep)
            if k == 1:
                adjoint[lev] = field
            else:
                for comp in range(3):
                    out[comp * LEV + lev] = field[comp][:ROWS]


def on_device(checkpoints, ckpt_index, innovations, seeds):
    slot = checkpoints.reshape(PLANES, ROWS, LON)
    current = innovations.reshape(2, PLANES, ROWS, LON)
    hbm = pl.BlockSpec(memory_space=pltpu.HBM)
    slot, current, ckpt_index = (
        pltpu.with_memory_space_constraint(operand, pltpu.HBM) for operand in (slot, current, ckpt_index)
    )
    field = (2, PLANES, ROWS, LON)
    dma = pltpu.SemaphoreType.DMA

    def vmem(*shape):
        return pltpu.VMEM(shape, jnp.float32)

    result = pl.pallas_call(
        kernel,
        out_shape=jax.ShapeDtypeStruct((PLANES, ROWS, LON), jnp.float32),
        in_specs=[hbm, pl.BlockSpec(memory_space=pltpu.SMEM), hbm, hbm],
        out_specs=pl.BlockSpec(memory_space=pltpu.VMEM),
        scratch_shapes=[
            pltpu.SMEM((2,), jnp.int32),
            vmem(PLANES, ROWS, LON),
            vmem(NY, HALF // 2, ROWS, 128),
            vmem(NZ, HALF // 2, ROWS, 128),
            vmem(HALF // 2, ROWS, 128),
            vmem(2, HALF // 2, ROWS, 128),
            vmem(HALF // 2, ROWS, 128),
            vmem(NZ, ROWS, LON),
            vmem(NY, ROWS, LON),
            vmem(ROWS, LON),
            vmem(2, ROWS, LON),
            vmem(ROWS, LON),
            vmem(PLANES, ROWS, LON),
            vmem(NY, HALF, ROWS, 128),
            vmem(NZ, HALF, ROWS, 128),
            vmem(HALF, ROWS, 128),
            vmem(2, HALF, ROWS, 128),
            vmem(*field),
            vmem(*field),
            vmem(*field),
            vmem(*field),
            dma((3, 2)),
            dma((3, 2)),
            dma((4, 2)),
            dma((2, 2, 2)),
            dma((2, 2)),
            dma((2, 2)),
            dma((2, 2)),
            dma((2, 2, 2)),
            dma((2, 2, 2)),
            dma((3,)),
        ],
        compiler_params=pltpu.CompilerParams(
            collective_id=0, has_side_effects=True, vmem_limit_bytes=32 * 2**20
        ),
        name="ensemble_adjoint",
    )(ckpt_index, seeds, slot, current)
    return result.reshape(1, 3, LEV, ROWS, LON)


def solution(mesh):
    return jax.shard_map(
        on_device,
        mesh=mesh,
        in_specs=(
            P("member", None, None, "band", None),
            P(),
            P(None, None, None, "band", None),
            P("member"),
        ),
        out_specs=P("member", None, None, "band", None),
        check_vma=False,
    )
```

```python
import functools

import jax
import jax.numpy as jnp
from jax import lax
from jax.experimental import pallas as pl
from jax.experimental.pallas import tpu as pltpu
from jax.sharding import PartitionSpec as P

NY = 8
NZ = 6
NBAND = 16
CHIPS = NBAND // 2
LEV = 4
PLANES = 3 * LEV
HALF = PLANES // 2
ROWS = 8
LON = 512
LAST_SLOT = NY * NZ - 1
EDGE = {1: 4, 0: 2}
MESH = pl.DeviceIdType.MESH


def next_lon(x):
    return pltpu.roll(x, LON - 1, 1)


def prev_lon(x):
    return pltpu.roll(x, 1, 1)


def next_row(x):
    return pltpu.roll(x, 2 * ROWS - 1, 0)


def prev_row(x):
    return pltpu.roll(x, 1, 0)


def advance(east, north, height):
    diff_east = 0.1 * (next_lon(east) - prev_lon(east))
    diff_north = 0.1 * (next_lon(north) - prev_lon(north))
    diff_height = 0.1 * (next_lon(height) - prev_lon(height))
    return (
        east - (east * diff_east + diff_height),
        north - east * diff_north,
        height - (east * diff_height + diff_east),
    )


def adjoint_step(state, adjoint, keep):
    east, north, height = state
    a, b, c = adjoint
    depth = 0.1 * jnp.exp(0.25 * height)
    visc = 0.04 + 0.02 * jnp.tanh(height)
    east, north = 0.1 * east, 0.1 * north
    c_next, c_prev = visc + east, visc - east
    r_next, r_prev = visc + north, visc - north
    middle = 1.0 - 4.0 * visc

    def spread(f, zonal=None, merid=None):
        if zonal is None:
            zonal = merid = 0.0
        return (
            middle * f
            + next_lon(c_next * f + zonal)
            + prev_lon(c_prev * f - zonal)
            + next_row(r_next * f + merid)
            + prev_row(r_prev * f - merid)
        )

    new_a = spread(a) + depth * (next_lon(c) - prev_lon(c))
    new_b = spread(b) + depth * (next_row(c) - prev_row(c))
    new_c = spread(c, 0.1 * a, 0.1 * b)
    return tuple(jnp.where(keep, f, 0.0) for f in (new_a, new_b, new_c))


def kernel(
    index_hbm, seed_ref, ckpt, innov, out,
    index_ref, slot,
    p_row, p_col, p_last, p_mine, p_edge,
    q_col, q_row, q_last, q_mine, q_edge,
    own, edge, force, force_edge,
    p_sem, q_sem, gather_sem, cross_sem, spread_sem, edge_sem, force_sem, local_sem,
):
    band = lax.axis_index("band")
    member = lax.axis_index("member")
    y, z = lax.rem(member, NY), member // NY
    chip = band // 2
    odd = lax.rem(band, 2) == 1
    even = jnp.logical_not(odd)
    has_up, has_down = band < NBAND - 1, band > 0
    chip_up, chip_down = chip < CHIPS - 1, chip > 0
    far_up, far_down = chip == CHIPS // 2 - 1, chip == CHIPS // 2
    z_above = jnp.where(far_up, NZ - 1 - z, z)
    z_below = jnp.where(far_down, NZ - 1 - z, z)
    member_up = z_above * NY + y
    member_down = z_below * NY + y

    y_peers = [lax.rem(y + step, NY) for step in range(1, NY)]
    z_peers = [lax.rem(z + step, NZ) for step in range(1, NZ)]
    low_band, high_band = 2 * chip, 2 * chip + 1

    def at_y(peer, of_band):
        return {"band": of_band, "member": z * NY + peer}

    def at_z(peer, of_band):
        return {"band": of_band, "member": peer * NY + y}

    sibling = {"band": low_band + high_band - band}
    up = {"band": band + 1, "member": jnp.where(odd, member_up, member)}
    down = {"band": band - 1, "member": jnp.where(odd, member, member_down)}
    handler_up = {"band": band + 2, "member": member_up}
    handler_down = {"band": band - 2, "member": member_down}

    def low_rows(k):
        return slice(0, EDGE[k])

    def high_rows(k):
        return slice(ROWS - EDGE[k], ROWS)

    def p_part(peer, rows=slice(None)):
        planes = pl.ds((HALF // 2) * (peer // 4), HALF // 2)
        return planes, rows, pl.ds(pl.multiple_of(128 * lax.rem(peer, 4), 128), 128)

    def q_part(peer, rows=slice(None)):
        return HALF + peer, rows

    def send(src, dst, sems, device):
        return pltpu.make_async_remote_copy(
            src_ref=src, dst_ref=dst, send_sem=sems.at[0], recv_sem=sems.at[1],
            device_id=device, device_id_type=MESH,
        )

    def drain(ref, sems):
        return send(ref, ref, sems, sibling)

    def p_pieces(count, rows=slice(None)):
        return p_row.at[pl.ds(0, count), :, rows]

    def q_planes(count, rows=slice(None)):
        return q_col.at[pl.ds(0, count), rows]

    def copy(src, dst, number):
        return pltpu.make_async_copy(src, dst, local_sem.at[number])

    barrier = pltpu.get_barrier_semaphore()

    def greet(device):
        pl.semaphore_signal(barrier, inc=1, device_id=device, device_id_type=MESH)

    for peer in z_peers:
        greet(at_z(peer, high_band))
    for peer in y_peers:
        greet(at_y(peer, high_band))
    greet(sibling)

    @pl.when(odd)
    def _():
        for peer in z_peers:
            greet(at_z(peer, low_band))
        for peer in y_peers:
            greet(at_y(peer, low_band))
        pl.when(chip_up)(lambda: greet(up))
        pl.when(chip_up)(lambda: greet(handler_up))
        pl.when(chip_down)(lambda: greet(handler_down))

    pl.when(jnp.logical_and(even, has_down))(lambda: greet(down))

    load_slot = copy(ckpt, slot, 0)
    load_index = copy(index_hbm, index_ref, 1)
    load_force = copy(innov, force, 2)
    load_slot.start()
    load_index.start()
    load_force.start()
    load_slot.wait()
    peers = NY + NZ - 2
    inner = jnp.logical_and(chip_up, chip_down)
    first, last = chip == 0, chip == CHIPS - 1
    for condition, count in (
        (jnp.logical_and(even, first), peers + 1),
        (jnp.logical_and(even, chip_down), peers + 2),
        (jnp.logical_and(odd, first), 2 * peers + 3),
        (jnp.logical_and(odd, last), 2 * peers + 2),
        (jnp.logical_and(odd, inner), 2 * peers + 4),
    ):
        pl.when(condition)(functools.partial(pl.semaphore_wait, barrier, count))

    def spots(core):
        return core * NZ + z, core * NY + y

    def first_phase(core):
        q_spot, p_spot = spots(core)
        for peer in z_peers:
            send(slot.at[q_part(peer)], q_col.at[q_spot], q_sem.at[0], at_z(peer, high_band)).start()
        for peer in y_peers:
            send(slot.at[p_part(peer)], p_row.at[p_spot], p_sem.at[0], at_y(peer, high_band)).start()
        if core == 0:
            send(slot.at[q_part(z)], q_col.at[q_spot], q_sem.at[0], sibling).start()
            send(slot.at[p_part(y)], p_row.at[p_spot], p_sem.at[0], sibling).start()
        else:
            p_row[p_spot] = slot[p_part(y)]
            q_col[q_spot] = slot[q_part(z)]

    pl.when(even)(lambda: first_phase(0))
    pl.when(odd)(lambda: first_phase(1))

    def edge_up(src, dst, sems, k, device):
        rows = (k, slice(None), high_rows(k))
        return send(src.at[rows], dst.at[rows], sems.at[k, 0], device)

    def edge_down(src, dst, sems, k, device):
        rows = (k, slice(None), low_rows(k))
        return send(src.at[rows], dst.at[rows], sems.at[k, 1], device)

    def start_edges(src, dst, sems, k, upward, downward):
        pl.when(upward)(lambda: edge_up(src, dst, sems, k, up).start())
        pl.when(downward)(lambda: edge_down(src, dst, sems, k, down).start())

    def finish_edges(src, dst, sems, k, upward, downward):
        def upper():
            edge_up(src, dst, sems, k, up).wait_send()
            edge_down(src, dst, sems, k, up).wait_recv()

        def lower():
            edge_down(src, dst, sems, k, down).wait_send()
            edge_up(src, dst, sems, k, down).wait_recv()

        pl.when(upward)(upper)
        pl.when(downward)(lower)

    for k in (1, 0):
        start_edges(innov, force_edge, force_sem, k, has_up, has_down)

    load_index.wait()
    seed = seed_ref[0]
    index = [index_ref[0], index_ref[1]]
    other = jnp.where(index[0] == LAST_SLOT, index[1], index[0])
    other_y, other_z = lax.rem(other, NY), other // NY
    load_force.wait()
    for k in range(2):
        for plane in range(PLANES):
            force[k, plane] = pltpu.roll(force[k, plane], seed, 1)

    @pl.when(odd)
    def _():
        drain(p_pieces(2 * NY - 1), p_sem.at[0]).wait_recv()
        for core in range(2):
            p_col[z, core] = p_row[core * NY + other_y]
        for peer in z_peers:
            send(p_col.at[z], p_col.at[z], p_sem.at[1], at_z(peer, high_band)).start()

        @pl.when(z == NZ - 1)
        def _():
            for core in range(2):
                p_last[core] = p_row[core * NY + NY - 1]
            for peer in z_peers:
                send(p_last, p_last, p_sem.at[2], at_z(peer, high_band)).start()

        drain(q_planes(2 * NZ - 1), q_sem.at[0]).wait_recv()
        for core in range(2):
            q_row[y, core] = q_col[core * NZ + other_z]
        for peer in y_peers:
            send(q_row.at[y], q_row.at[y], q_sem.at[1], at_y(peer, high_band)).start()

        @pl.when(y == NY - 1)
        def _():
            for core in range(2):
                q_last[core] = q_col[core * NZ + NZ - 1]
            for peer in y_peers:
                send(q_last, q_last, q_sem.at[2], at_y(peer, high_band)).start()

        def cross_up(mine, landing, kind, k, rows):
            return send(
                mine.at[(k, 1) + rows(high_rows(k))], landing.at[(1, k) + rows(high_rows(k))],
                cross_sem.at[0, kind, k], handler_up,
            )

        def cross_down(mine, landing, kind, k, rows):
            return send(
                mine.at[(k, 0) + rows(low_rows(k))], landing.at[(0, k) + rows(low_rows(k))],
                cross_sem.at[1, kind, k], handler_down,
            )

        def p_rows(rows):
            return slice(None), rows

        def q_rows(rows):
            return (rows,)

        def start_cross(*job):
            pl.when(chip_up)(lambda: cross_up(*job).start())
            pl.when(chip_down)(lambda: cross_down(*job).start())

        drain(p_col.at[pl.ds(0, NZ - 1)], p_sem.at[1]).wait()
        pl.when(z == NZ - 1)(lambda: drain(p_col.at[pl.ds(0, NZ - 1)], p_sem.at[2]).wait_send())
        pl.when(z < NZ - 1)(lambda: drain(p_last, p_sem.at[2]).wait_recv())
        from_other, from_last = p_col[other_z], p_last[...]
        for k in (1, 0):
            p_mine[k] = jnp.where(index[k] == LAST_SLOT, from_last, from_other)
            start_cross(p_mine, p_edge, 0, k, p_rows)
        for k in (1, 0):
            place = (k,) + p_part(y)
            send(p_mine.at[k, 0], own.at[place], gather_sem.at[k, 0], sibling).start()
            for peer in y_peers:
                send(p_mine.at[k, 0], own.at[place], gather_sem.at[k, 0], at_y(peer, low_band)).start()
                send(p_mine.at[k, 1], own.at[place], gather_sem.at[k, 0], at_y(peer, high_band)).start()
            own[place] = p_mine[k, 1]

        drain(q_row.at[pl.ds(0, NY - 1)], q_sem.at[1]).wait()
        pl.when(y == NY - 1)(lambda: drain(q_row.at[pl.ds(0, NY - 1)], q_sem.at[2]).wait_send())
        pl.when(y < NY - 1)(lambda: drain(q_last, q_sem.at[2]).wait_recv())
        from_other, from_last = q_row[other_y], q_last[...]
        for k in (1, 0):
            q_mine[k] = jnp.where(index[k] == LAST_SLOT, from_last, from_other)
            start_cross(q_mine, q_edge, 1, k, q_rows)
        for k in (1, 0):
            place = (k,) + q_part(z)
            send(q_mine.at[k, 0], own.at[place], gather_sem.at[k, 1], sibling).start()
            for peer in z_peers:
                send(q_mine.at[k, 0], own.at[place], gather_sem.at[k, 1], at_z(peer, low_band)).start()
                send(q_mine.at[k, 1], own.at[place], gather_sem.at[k, 1], at_z(peer, high_band)).start()
            own[place] = q_mine[k, 1]

        def spread_p(k):
            @pl.when(chip_down)
            def _():
                cross_up(p_mine, p_edge, 0, k, p_rows).wait_recv()
                piece, place = p_edge.at[1, k, :, high_rows(k)], (k,) + p_part(y, high_rows(k))
                send(piece, edge.at[place], spread_sem.at[0, k, 0], sibling).start()
                for peer in y_peers:
                    send(piece, edge.at[place], spread_sem.at[0, k, 0], at_y(peer, low_band)).start()

            @pl.when(chip_up)
            def _():
                cross_down(p_mine, p_edge, 0, k, p_rows).wait_recv()
                piece, place = p_edge.at[0, k, :, low_rows(k)], (k,) + p_part(y, low_rows(k))
                for peer in y_peers:
                    send(piece, edge.at[place], spread_sem.at[1, k, 0], at_y(peer, high_band)).start()
                edge[place] = p_edge[0, k, :, low_rows(k)]

        def spread_q(k):
            @pl.when(chip_down)
            def _():
                cross_up(q_mine, q_edge, 1, k, q_rows).wait_recv()
                piece, place = q_edge.at[1, k, high_rows(k)], (k,) + q_part(z_below, high_rows(k))
                send(piece, edge.at[place], spread_sem.at[0, k, 1], sibling).start()
                for peer in z_peers:
                    send(piece, edge.at[place], spread_sem.at[0, k, 1], at_z(peer, low_band)).start()

            @pl.when(chip_up)
            def _():
                cross_down(q_mine, q_edge, 1, k, q_rows).wait_recv()
                piece, place = q_edge.at[0, k, low_rows(k)], (k,) + q_part(z_above, low_rows(k))
                for peer in z_peers:
                    send(piece, edge.at[place], spread_sem.at[1, k, 1], at_z(peer, high_band)).start()
                edge[place] = q_edge[0, k, low_rows(k)]

        for k in (1, 0):
            spread_p(k)
        for k in (1, 0):
            spread_q(k)

    for k in (1, 0):
        finish_edges(innov, force_edge, force_sem, k, has_up, has_down)
        for plane in range(PLANES):
            force_edge[k, plane] = pltpu.roll(force_edge[k, plane], seed, 1)

    for k in (1, 0):
        @pl.when(odd)
        def _():
            drain(p_pieces(NY - 1), gather_sem.at[k, 0]).wait_recv()
            drain(q_planes(NZ - 1), gather_sem.at[k, 1]).wait_recv()

        @pl.when(even)
        def _():
            drain(p_pieces(NY), gather_sem.at[k, 0]).wait_recv()
            drain(q_planes(NZ), gather_sem.at[k, 1]).wait_recv()

        start_edges(own, edge, edge_sem, k, even, odd)

    row = lax.broadcasted_iota(jnp.int32, (ROWS, LON), 0)
    inside = jnp.logical_not(
        jnp.logical_or(
            jnp.logical_and(band == NBAND - 1, row < ROWS // 2),
            jnp.logical_and(band == 0, row >= ROWS // 2),
        )
    )
    keep = jnp.logical_or(
        lax.broadcasted_iota(jnp.int32, (2 * ROWS, LON), 0) < ROWS,
        jnp.concatenate([inside, inside], axis=0),
    )

    adjoint = [None] * LEV
    for k in (1, 0):
        @pl.when(jnp.logical_and(even, chip_down))
        def _():
            drain(p_pieces(NY, high_rows(k)), spread_sem.at[0, k, 0]).wait_recv()
            drain(q_planes(NZ, high_rows(k)), spread_sem.at[0, k, 1]).wait_recv()

        @pl.when(jnp.logical_and(odd, chip_up))
        def _():
            drain(p_pieces(NY - 1, low_rows(k)), spread_sem.at[1, k, 0]).wait_recv()
            drain(q_planes(NZ - 1, low_rows(k)), spread_sem.at[1, k, 1]).wait_recv()

        finish_edges(own, edge, edge_sem, k, even, odd)
        for lev in range(LEV):
            def both(inner_ref, outer_ref):
                return tuple(
                    jnp.concatenate(
                        [
                            inner_ref[k, comp * LEV + lev],
                            jnp.where(inside, outer_ref[k, comp * LEV + lev], 0.0),
                        ],
                        axis=0,
                    )
                    for comp in range(3)
                )

            forcing = both(force, force_edge)
            if adjoint[lev] is None:
                field = forcing
            else:
                field = tuple(f + g for f, g in zip(adjoint[lev], forcing))
            start = both(own, edge)
            field = adjoint_step(advance(*start), field, keep)
            field = adjoint_step(start, field, keep)
            if k == 1:
                adjoint[lev] = field
            else:
                for comp in range(3):
                    out[comp * LEV + lev] = field[comp][:ROWS]

    @pl.when(even)
    def _():
        drain(p_pieces(NY), p_sem.at[0]).wait_send()
        drain(q_planes(NZ), q_sem.at[0]).wait_send()

    @pl.when(odd)
    def _():
        drain(p_pieces(NY - 1), p_sem.at[0]).wait_send()
        drain(q_planes(NZ - 1), q_sem.at[0]).wait_send()
        for k in (1, 0):
            drain(p_pieces(2 * NY - 1), gather_sem.at[k, 0]).wait_send()
            drain(q_planes(2 * NZ - 1), gather_sem.at[k, 1]).wait_send()

            @pl.when(chip_up)
            def _():
                drain(p_edge.at[0, k, :, high_rows(k)], cross_sem.at[0, 0, k]).wait_send()
                drain(q_edge.at[0, k, high_rows(k)], cross_sem.at[0, 1, k]).wait_send()
                drain(p_pieces(NY - 1, low_rows(k)), spread_sem.at[1, k, 0]).wait_send()
                drain(q_planes(NZ - 1, low_rows(k)), spread_sem.at[1, k, 1]).wait_send()

            @pl.when(chip_down)
            def _():
                drain(p_edge.at[0, k, :, low_rows(k)], cross_sem.at[1, 0, k]).wait_send()
                drain(q_edge.at[0, k, low_rows(k)], cross_sem.at[1, 1, k]).wait_send()
                drain(p_pieces(NY, high_rows(k)), spread_sem.at[0, k, 0]).wait_send()
                drain(q_planes(NZ, high_rows(k)), spread_sem.at[0, k, 1]).wait_send()


def on_device(checkpoints, ckpt_index, innovations, seeds):
    slot = checkpoints.reshape(PLANES, ROWS, LON)
    current = innovations.reshape(2, PLANES, ROWS, LON)
    hbm = pl.BlockSpec(memory_space=pltpu.HBM)
    slot, current, ckpt_index = (
        pltpu.with_memory_space_constraint(operand, pltpu.HBM) for operand in (slot, current, ckpt_index)
    )
    field = (2, PLANES, ROWS, LON)
    dma = pltpu.SemaphoreType.DMA

    def vmem(*shape):
        return pltpu.VMEM(shape, jnp.float32)

    result = pl.pallas_call(
        kernel,
        out_shape=jax.ShapeDtypeStruct((PLANES, ROWS, LON), jnp.float32),
        in_specs=[hbm, pl.BlockSpec(memory_space=pltpu.SMEM), hbm, hbm],
        out_specs=pl.BlockSpec(memory_space=pltpu.VMEM),
        scratch_shapes=[
            pltpu.SMEM((2,), jnp.int32),
            vmem(PLANES, ROWS, LON),
            vmem(2 * NY, HALF // 2, ROWS, 128),
            vmem(NZ, 2, HALF // 2, ROWS, 128),
            vmem(2, HALF // 2, ROWS, 128),
            vmem(2, 2, HALF // 2, ROWS, 128),
            vmem(2, 2, HALF // 2, ROWS, 128),
            vmem(2 * NZ, ROWS, LON),
            vmem(NY, 2, ROWS, LON),
            vmem(2, ROWS, LON),
            vmem(2, 2, ROWS, LON),
            vmem(2, 2, ROWS, LON),
            vmem(*field),
            vmem(*field),
            vmem(*field),
            vmem(*field),
            dma((3, 2)),
            dma((3, 2)),
            dma((2, 2, 2)),
            dma((2, 2, 2, 2)),
            dma((2, 2, 2, 2)),
            dma((2, 2, 2)),
            dma((2, 2, 2)),
            dma((3,)),
        ],
        compiler_params=pltpu.CompilerParams(
            collective_id=0, has_side_effects=True, vmem_limit_bytes=32 * 2**20
        ),
        name="ensemble_adjoint",
    )(ckpt_index, seeds, slot, current)
    return result.reshape(1, 3, LEV, ROWS, LON)


def solution(mesh):
    return jax.shard_map(
        on_device,
        mesh=mesh,
        in_specs=(
            P("member", None, None, "band", None),
            P(),
            P(None, None, None, "band", None),
            P("member"),
        ),
        out_specs=P("member", None, None, "band", None),
        check_vma=False,
    )
```

```python
import functools

import jax
import jax.numpy as jnp
from jax import lax
from jax.experimental import pallas as pl
from jax.experimental.pallas import tpu as pltpu
from jax.sharding import PartitionSpec as P

NY = 8
NZ = 6
NBAND = 16
CHIPS = NBAND // 2
LEV = 4
PLANES = 3 * LEV
HALF = PLANES // 2
ROWS = 8
LON = 512
LAST_SLOT = NY * NZ - 1
EDGE = {1: 4, 0: 2}
P_CHUNKS, Q_CHUNKS = HALF // 2, 4
WIDTH = LON // Q_CHUNKS
MESH = pl.DeviceIdType.MESH


def next_lon(x):
    return pltpu.roll(x, LON - 1, 1)


def prev_lon(x):
    return pltpu.roll(x, 1, 1)


def next_row(x):
    return pltpu.roll(x, 2 * ROWS - 1, 0)


def prev_row(x):
    return pltpu.roll(x, 1, 0)


def advance(east, north, height):
    diff_east = 0.1 * (next_lon(east) - prev_lon(east))
    diff_north = 0.1 * (next_lon(north) - prev_lon(north))
    diff_height = 0.1 * (next_lon(height) - prev_lon(height))
    return (
        east - (east * diff_east + diff_height),
        north - east * diff_north,
        height - (east * diff_height + diff_east),
    )


def coefficients(state):
    east, north, height = state
    depth = 0.1 * jnp.exp(0.25 * height)
    visc = 0.04 + 0.02 * jnp.tanh(height)
    east, north = 0.1 * east, 0.1 * north
    return depth, 1.0 - 4.0 * visc, visc + east, visc - east, visc + north, visc - north


def adjoint_step(factors, adjoint, keep):
    depth, middle, c_next, c_prev, r_next, r_prev = factors
    a, b, c = adjoint

    def spread(f, zonal=None, merid=None):
        if zonal is None:
            zonal = merid = 0.0
        return (
            middle * f
            + next_lon(c_next * f + zonal)
            + prev_lon(c_prev * f - zonal)
            + next_row(r_next * f + merid)
            + prev_row(r_prev * f - merid)
        )

    new_a = spread(a) + depth * (next_lon(c) - prev_lon(c))
    new_b = spread(b) + depth * (next_row(c) - prev_row(c))
    new_c = spread(c, 0.1 * a, 0.1 * b)
    return tuple(jnp.where(keep, f, 0.0) for f in (new_a, new_b, new_c))


def kernel(
    index_hbm, seed_ref, ckpt, innov, out,
    index_ref, slot,
    p_meter, p_rows_in, p_cols_in, p_last, p_mine, p_edge,
    q_meter, q_cols_in, q_rows_in, q_last, q_mine, q_edge,
    own, edge, force, force_edge, factor,
    p_sem, q_sem, gather_sem, cross_sem, spread_sem, edge_sem, force_sem, local_sem, ready_sem,
):
    band = lax.axis_index("band")
    member = lax.axis_index("member")
    y, z = lax.rem(member, NY), member // NY
    chip = band // 2
    odd = lax.rem(band, 2) == 1
    even = jnp.logical_not(odd)
    has_up, has_down = band < NBAND - 1, band > 0
    chip_up = chip < CHIPS - 1
    far_up, far_down = chip == CHIPS // 2 - 1, chip == CHIPS // 2
    near_up = jnp.logical_and(has_up, band != CHIPS - 1)
    near_down = jnp.logical_and(has_down, band != CHIPS)
    z_above = jnp.where(far_up, NZ - 1 - z, z)
    z_below = jnp.where(far_down, NZ - 1 - z, z)
    member_up = z_above * NY + y
    member_down = z_below * NY + y

    y_peers = [lax.rem(y + step, NY) for step in range(1, NY)]
    z_peers = [lax.rem(z + step, NZ) for step in range(1, NZ)]
    low_band, high_band = 2 * chip, 2 * chip + 1

    def at_y(peer, of_band):
        return {"band": of_band, "member": z * NY + peer}

    def at_z(peer, of_band):
        return {"band": of_band, "member": peer * NY + y}

    sibling = {"band": low_band + high_band - band}
    up = {"band": band + 1, "member": jnp.where(odd, member_up, member)}
    down = {"band": band - 1, "member": jnp.where(odd, member, member_down)}
    handler_up = {"band": band + 2, "member": member_up}
    handler_down = {"band": band - 2, "member": member_down}

    def low_rows(k):
        return slice(0, EDGE[k])

    def high_rows(k):
        return slice(ROWS - EDGE[k], ROWS)

    def p_part(peer, rows=slice(None)):
        planes = pl.ds((HALF // 2) * (peer // 4), HALF // 2)
        return planes, rows, pl.ds(pl.multiple_of(128 * lax.rem(peer, 4), 128), 128)

    def q_part(peer, rows=slice(None)):
        return HALF + peer, rows

    def p_chunk(peer, i):
        lanes = pl.ds(pl.multiple_of(128 * lax.rem(peer, 4), 128), 128)
        return P_CHUNKS * (peer // 4) + i, slice(None), lanes

    def q_lanes(i):
        return slice(WIDTH * i, WIDTH * (i + 1))

    def q_chunk(peer, i):
        return HALF + peer, slice(None), q_lanes(i)

    def send(src, dst, sems, device):
        return pltpu.make_async_remote_copy(
            src_ref=src, dst_ref=dst, send_sem=sems.at[0], recv_sem=sems.at[1],
            device_id=device, device_id_type=MESH,
        )

    def drain(ref, sems):
        return send(ref, ref, sems, sibling)

    def p_pieces(count, rows=slice(None)):
        return p_meter.at[:, pl.ds(0, count), rows]

    def q_planes(count, rows=slice(None)):
        return q_meter.at[:, pl.ds(0, count), rows]

    def copy(src, dst, number):
        return pltpu.make_async_copy(src, dst, local_sem.at[number])

    barrier = pltpu.get_barrier_semaphore()

    def greet(device):
        pl.semaphore_signal(barrier, inc=1, device_id=device, device_id_type=MESH)

    for peer in z_peers:
        greet(at_z(peer, high_band))
    for peer in y_peers:
        greet(at_y(peer, high_band))
    greet(sibling)

    @pl.when(odd)
    def _():
        for peer in z_peers:
            greet(at_z(peer, low_band))
        for peer in y_peers:
            greet(at_y(peer, low_band))
        pl.when(chip_up)(lambda: greet(up))
        pl.when(far_up)(lambda: greet(handler_up))

    pl.when(jnp.logical_and(even, near_down))(lambda: greet(down))

    load_slot = copy(ckpt, slot, 0)
    load_index = copy(index_hbm, index_ref, 1)
    load_force = copy(innov, force, 2)
    load_slot.start()
    load_index.start()
    load_force.start()
    load_slot.wait()
    peers = NY + NZ - 2
    alone = jnp.logical_or(far_up, chip == CHIPS - 1)
    plain = jnp.logical_not(jnp.logical_or(alone, far_down))
    for condition, count in (
        (band == 0, peers + 1),
        (jnp.logical_and(even, has_down), peers + 2),
        (jnp.logical_and(odd, alone), 2 * peers + 1),
        (jnp.logical_and(odd, plain), 2 * peers + 2),
        (jnp.logical_and(odd, far_down), 2 * peers + 3),
    ):
        pl.when(condition)(functools.partial(pl.semaphore_wait, barrier, count))

    def tell(number, device):
        pl.semaphore_signal(ready_sem.at[number], inc=1, device_id=device, device_id_type=MESH)

    pl.when(jnp.logical_and(even, far_down))(lambda: tell(0, down))
    pl.when(jnp.logical_and(odd, far_down))(lambda: tell(1, handler_down))

    def spots(core):
        return core * NZ + z, core * NY + y

    streams = [("q", 0), ("p", 0), ("q", 1), ("p", 1), ("q", 2), ("p", 2), ("q", 3)]

    def first_phase(core):
        q_spot, p_spot = spots(core)
        for kind, i in streams:
            if kind == "p":
                for peer in y_peers:
                    send(slot.at[p_chunk(peer, i)], p_rows_in[i].at[p_spot], p_sem.at[0, i], at_y(peer, high_band)).start()
                if core == 0:
                    send(slot.at[p_chunk(y, i)], p_rows_in[i].at[p_spot], p_sem.at[0, i], sibling).start()
                else:
                    p_rows_in[i][p_spot] = slot[p_chunk(y, i)]
            else:
                for peer in z_peers:
                    send(slot.at[q_chunk(peer, i)], q_cols_in[i].at[q_spot], q_sem.at[0, i], at_z(peer, high_band)).start()
                if core == 0:
                    send(slot.at[q_chunk(z, i)], q_cols_in[i].at[q_spot], q_sem.at[0, i], sibling).start()
                else:
                    q_cols_in[i][q_spot] = slot[q_chunk(z, i)]

    pl.when(even)(lambda: first_phase(0))
    pl.when(odd)(lambda: first_phase(1))

    everything, p_planes, q_planes_all = slice(0, PLANES), slice(0, HALF), slice(HALF, PLANES)

    def edge_up(src, dst, sems, k, planes, device):
        rows = (k, planes, high_rows(k))
        return send(src.at[rows], dst.at[rows], sems.at[k, 0], device)

    def edge_down(src, dst, sems, k, planes, device):
        rows = (k, planes, low_rows(k))
        return send(src.at[rows], dst.at[rows], sems.at[k, 1], device)

    def start_edges(src, dst, sems, k, planes, upward, downward):
        pl.when(upward)(lambda: edge_up(src, dst, sems, k, planes, up).start())
        pl.when(downward)(lambda: edge_down(src, dst, sems, k, planes, down).start())

    def finish_edges(src, dst, sems, k, planes, upward, downward):
        def upper():
            edge_up(src, dst, sems, k, planes, up).wait_send()
            edge_down(src, dst, sems, k, planes, up).wait_recv()

        def lower():
            edge_down(src, dst, sems, k, planes, down).wait_send()
            edge_up(src, dst, sems, k, planes, down).wait_recv()

        pl.when(upward)(upper)
        pl.when(downward)(lower)

    for k in (1, 0):
        start_edges(innov, force_edge, force_sem, k, everything, near_up, has_down)

    load_index.wait()
    seed = seed_ref[0]
    index = [index_ref[0], index_ref[1]]
    other = jnp.where(index[0] == LAST_SLOT, index[1], index[0])
    other_y, other_z = lax.rem(other, NY), other // NY
    load_force.wait()
    for k in range(2):
        for plane in range(PLANES):
            force[k, plane] = pltpu.roll(force[k, plane], seed, 1)

    @pl.when(odd)
    def _():
        for kind, i in streams:
            if kind == "p":
                drain(p_rows_in[i].at[pl.ds(0, 2 * NY - 1)], p_sem.at[0, i]).wait_recv()
                for core in range(2):
                    p_cols_in[i][z, core] = p_rows_in[i][core * NY + other_y]
                for peer in z_peers:
                    send(p_cols_in[i].at[z], p_cols_in[i].at[z], p_sem.at[1, i], at_z(peer, high_band)).start()

                @pl.when(z == NZ - 1)
                def _():
                    for core in range(2):
                        p_last[i, core] = p_rows_in[i][core * NY + NY - 1]
                    for peer in z_peers:
                        send(p_last.at[i], p_last.at[i], p_sem.at[2, i], at_z(peer, high_band)).start()
            else:
                drain(q_cols_in[i].at[pl.ds(0, 2 * NZ - 1)], q_sem.at[0, i]).wait_recv()
                for core in range(2):
                    q_rows_in[i][y, core] = q_cols_in[i][core * NZ + other_z]
                for peer in y_peers:
                    send(q_rows_in[i].at[y], q_rows_in[i].at[y], q_sem.at[1, i], at_y(peer, high_band)).start()

                @pl.when(y == NY - 1)
                def _():
                    for core in range(2):
                        q_last[i, core] = q_cols_in[i][core * NZ + NZ - 1]
                    for peer in y_peers:
                        send(q_last.at[i], q_last.at[i], q_sem.at[2, i], at_y(peer, high_band)).start()

        def cross_up(mine, landing, kind, k, rows):
            return send(
                mine.at[(k, 1) + rows(high_rows(k))], landing.at[(1, k) + rows(high_rows(k))],
                cross_sem.at[0, kind, k], handler_up,
            )

        def cross_down(mine, landing, kind, k, rows):
            return send(
                mine.at[(k, 0) + rows(low_rows(k))], landing.at[(0, k) + rows(low_rows(k))],
                cross_sem.at[1, kind, k], handler_down,
            )

        def p_rows(rows):
            return slice(None), rows

        def q_rows(rows):
            return (rows,)

        def start_cross(*job):
            pl.when(far_up)(lambda: cross_up(*job).start())
            pl.when(far_down)(lambda: cross_down(*job).start())

        for kind, i in streams:
            if kind == "p":
                drain(p_cols_in[i].at[pl.ds(0, NZ - 1)], p_sem.at[1, i]).wait()
                pl.when(z == NZ - 1)(lambda: drain(p_cols_in[i].at[pl.ds(0, NZ - 1)], p_sem.at[2, i]).wait_send())
                pl.when(z < NZ - 1)(lambda: drain(p_last.at[i], p_sem.at[2, i]).wait_recv())
                from_other, from_last = p_cols_in[i][other_z], p_last[i]
                for k in (1, 0):
                    p_mine[k, :, i] = jnp.where(index[k] == LAST_SLOT, from_last, from_other)
                place = (slice(None),) + p_chunk(y, i)
                send(p_mine.at[:, 0, i], own.at[place], gather_sem.at[0, 0], sibling).start()
                for peer in y_peers:
                    send(p_mine.at[:, 0, i], own.at[place], gather_sem.at[0, 0], at_y(peer, low_band)).start()
                    send(p_mine.at[:, 1, i], own.at[place], gather_sem.at[1, 0], at_y(peer, high_band)).start()
                if i == P_CHUNKS - 1:
                    @pl.when(far_up)
                    def _():
                        pl.semaphore_wait(ready_sem.at[0], 1)
                        pl.semaphore_wait(ready_sem.at[1], 1)
                        for k in (1, 0):
                            edge_up(innov, force_edge, force_sem, k, everything, up).start()

                for k in (1, 0):
                    own[(k,) + p_chunk(y, i)] = p_mine[k, 1, i]
                    if i == P_CHUNKS - 1:
                        start_cross(p_mine, p_edge, 0, k, p_rows)
            else:
                drain(q_rows_in[i].at[pl.ds(0, NY - 1)], q_sem.at[1, i]).wait()
                pl.when(y == NY - 1)(lambda: drain(q_rows_in[i].at[pl.ds(0, NY - 1)], q_sem.at[2, i]).wait_send())
                pl.when(y < NY - 1)(lambda: drain(q_last.at[i], q_sem.at[2, i]).wait_recv())
                from_other, from_last = q_rows_in[i][other_y], q_last[i]
                for k in (1, 0):
                    q_mine[k, :, :, q_lanes(i)] = jnp.where(index[k] == LAST_SLOT, from_last, from_other)
                place = (slice(None),) + q_chunk(z, i)
                send(q_mine.at[:, 0, :, q_lanes(i)], own.at[place], gather_sem.at[0, 1], sibling).start()
                for peer in z_peers:
                    send(q_mine.at[:, 0, :, q_lanes(i)], own.at[place], gather_sem.at[0, 1], at_z(peer, low_band)).start()
                    send(q_mine.at[:, 1, :, q_lanes(i)], own.at[place], gather_sem.at[1, 1], at_z(peer, high_band)).start()
                for k in (1, 0):
                    own[(k,) + q_chunk(z, i)] = q_mine[k, 1, :, q_lanes(i)]
                    if i == Q_CHUNKS - 1:
                        start_cross(q_mine, q_edge, 1, k, q_rows)

        def spread_p(k):
            @pl.when(far_down)
            def _():
                cross_up(p_mine, p_edge, 0, k, p_rows).wait_recv()
                piece, place = p_edge.at[1, k, :, high_rows(k)], (k,) + p_part(y, high_rows(k))
                send(piece, edge.at[place], spread_sem.at[0, k, 0], sibling).start()
                for peer in y_peers:
                    send(piece, edge.at[place], spread_sem.at[0, k, 0], at_y(peer, low_band)).start()

            @pl.when(far_up)
            def _():
                cross_down(p_mine, p_edge, 0, k, p_rows).wait_recv()
                piece, place = p_edge.at[0, k, :, low_rows(k)], (k,) + p_part(y, low_rows(k))
                for peer in y_peers:
                    send(piece, edge.at[place], spread_sem.at[1, k, 0], at_y(peer, high_band)).start()
                edge[place] = p_edge[0, k, :, low_rows(k)]

        def spread_q(k):
            @pl.when(far_down)
            def _():
                cross_up(q_mine, q_edge, 1, k, q_rows).wait_recv()
                piece, place = q_edge.at[1, k, high_rows(k)], (k,) + q_part(z_below, high_rows(k))
                send(piece, edge.at[place], spread_sem.at[0, k, 1], sibling).start()
                for peer in z_peers:
                    send(piece, edge.at[place], spread_sem.at[0, k, 1], at_z(peer, low_band)).start()

            @pl.when(far_up)
            def _():
                cross_down(q_mine, q_edge, 1, k, q_rows).wait_recv()
                piece, place = q_edge.at[0, k, low_rows(k)], (k,) + q_part(z_above, low_rows(k))
                for peer in z_peers:
                    send(piece, edge.at[place], spread_sem.at[1, k, 1], at_z(peer, high_band)).start()
                edge[place] = q_edge[0, k, low_rows(k)]

        for k in (1, 0):
            spread_p(k)
        for k in (1, 0):
            spread_q(k)

    def gathered(part, pieces, planes):
        pl.when(odd)(lambda: drain(pieces[0], gather_sem.at[1, part]).wait_recv())
        pl.when(even)(lambda: drain(pieces[1], gather_sem.at[0, part]).wait_recv())
        for k in (1, 0):
            start_edges(own, edge, edge_sem.at[part], k, planes, near_up, near_down)

    def factors_of(state):
        return coefficients(advance(*state)), coefficients(state)

    gathered(0, (p_pieces(2 * NY - 2), p_pieces(2 * NY)), p_planes)
    gathered(1, (q_planes(2 * NZ - 2), q_planes(2 * NZ)), q_planes_all)

    row = lax.broadcasted_iota(jnp.int32, (ROWS, LON), 0)
    inside = jnp.logical_not(
        jnp.logical_or(
            jnp.logical_and(band == NBAND - 1, row < ROWS // 2),
            jnp.logical_and(band == 0, row >= ROWS // 2),
        )
    )
    keep = jnp.logical_or(
        lax.broadcasted_iota(jnp.int32, (2 * ROWS, LON), 0) < ROWS,
        jnp.concatenate([inside, inside], axis=0),
    )

    for k in (1, 0):
        finish_edges(innov, force_edge, force_sem, k, everything, has_up, has_down)
        for plane in range(PLANES):
            force_edge[k, plane] = pltpu.roll(force_edge[k, plane], seed, 1)

    for k in (1, 0):
        for lev in range(LEV):
            state = tuple(own[k, comp * LEV + lev] for comp in range(3))
            for step, values in enumerate(factors_of(state)):
                for number, value in enumerate(values):
                    factor[k, lev, step, number] = value

    adjoint = [None] * LEV
    for k in (1, 0):
        @pl.when(jnp.logical_and(even, far_down))
        def _():
            drain(p_pieces(NY, high_rows(k)), spread_sem.at[0, k, 0]).wait_recv()
            drain(q_planes(NZ, high_rows(k)), spread_sem.at[0, k, 1]).wait_recv()

        @pl.when(jnp.logical_and(odd, far_up))
        def _():
            drain(p_pieces(NY - 1, low_rows(k)), spread_sem.at[1, k, 0]).wait_recv()
            drain(q_planes(NZ - 1, low_rows(k)), spread_sem.at[1, k, 1]).wait_recv()

        finish_edges(own, edge, edge_sem.at[0], k, p_planes, near_up, near_down)
        finish_edges(own, edge, edge_sem.at[1], k, q_planes_all, near_up, near_down)
        for lev in range(LEV):
            def both(inner_ref, outer_ref):
                return tuple(
                    jnp.concatenate(
                        [
                            inner_ref[k, comp * LEV + lev],
                            jnp.where(inside, outer_ref[k, comp * LEV + lev], 0.0),
                        ],
                        axis=0,
                    )
                    for comp in range(3)
                )

            forcing = both(force, force_edge)
            if adjoint[lev] is None:
                field = forcing
            else:
                field = tuple(f + g for f, g in zip(adjoint[lev], forcing))
            outer = tuple(jnp.where(inside, edge[k, comp * LEV + lev], 0.0) for comp in range(3))
            for step, values in enumerate(factors_of(outer)):
                whole = tuple(
                    jnp.concatenate([factor[k, lev, step, number], value], axis=0)
                    for number, value in enumerate(values)
                )
                field = adjoint_step(whole, field, keep)
            if k == 1:
                adjoint[lev] = field
            else:
                for comp in range(3):
                    out[comp * LEV + lev] = field[comp][:ROWS]

    def first_left(p_count, q_count):
        for i in range(P_CHUNKS):
            drain(p_rows_in[i].at[pl.ds(0, p_count)], p_sem.at[0, i]).wait_send()
        for i in range(Q_CHUNKS):
            drain(q_cols_in[i].at[pl.ds(0, q_count)], q_sem.at[0, i]).wait_send()

    pl.when(even)(lambda: first_left(NY, NZ))

    @pl.when(odd)
    def _():
        first_left(NY - 1, NZ - 1)
        drain(p_pieces(2 * NY), gather_sem.at[0, 0]).wait_send()
        drain(p_pieces(2 * NY - 2), gather_sem.at[1, 0]).wait_send()
        drain(q_planes(2 * NZ), gather_sem.at[0, 1]).wait_send()
        drain(q_planes(2 * NZ - 2), gather_sem.at[1, 1]).wait_send()
        for k in (1, 0):
            @pl.when(far_up)
            def _():
                drain(p_edge.at[0, k, :, high_rows(k)], cross_sem.at[0, 0, k]).wait_send()
                drain(q_edge.at[0, k, high_rows(k)], cross_sem.at[0, 1, k]).wait_send()
                drain(p_pieces(NY - 1, low_rows(k)), spread_sem.at[1, k, 0]).wait_send()
                drain(q_planes(NZ - 1, low_rows(k)), spread_sem.at[1, k, 1]).wait_send()

            @pl.when(far_down)
            def _():
                drain(p_edge.at[0, k, :, low_rows(k)], cross_sem.at[1, 0, k]).wait_send()
                drain(q_edge.at[0, k, low_rows(k)], cross_sem.at[1, 1, k]).wait_send()
                drain(p_pieces(NY, high_rows(k)), spread_sem.at[0, k, 0]).wait_send()
                drain(q_planes(NZ, high_rows(k)), spread_sem.at[0, k, 1]).wait_send()


def on_device(checkpoints, ckpt_index, innovations, seeds):
    slot = checkpoints.reshape(PLANES, ROWS, LON)
    current = innovations.reshape(2, PLANES, ROWS, LON)
    hbm = pl.BlockSpec(memory_space=pltpu.HBM)
    slot, current, ckpt_index = (
        pltpu.with_memory_space_constraint(operand, pltpu.HBM) for operand in (slot, current, ckpt_index)
    )
    field = (2, PLANES, ROWS, LON)
    dma = pltpu.SemaphoreType.DMA

    def vmem(*shape):
        return pltpu.VMEM(shape, jnp.float32)

    result = pl.pallas_call(
        kernel,
        out_shape=jax.ShapeDtypeStruct((PLANES, ROWS, LON), jnp.float32),
        in_specs=[hbm, pl.BlockSpec(memory_space=pltpu.SMEM), hbm, hbm],
        out_specs=pl.BlockSpec(memory_space=pltpu.VMEM),
        scratch_shapes=[
            pltpu.SMEM((2,), jnp.int32),
            vmem(PLANES, ROWS, LON),
            vmem(P_CHUNKS, 2 * NY, ROWS, 128),
            [vmem(2 * NY, ROWS, 128)] * P_CHUNKS,
            [vmem(NZ, 2, ROWS, 128)] * P_CHUNKS,
            vmem(P_CHUNKS, 2, ROWS, 128),
            vmem(2, 2, P_CHUNKS, ROWS, 128),
            vmem(2, 2, P_CHUNKS, ROWS, 128),
            vmem(Q_CHUNKS, 2 * NZ, ROWS, WIDTH),
            [vmem(2 * NZ, ROWS, WIDTH)] * Q_CHUNKS,
            [vmem(NY, 2, ROWS, WIDTH)] * Q_CHUNKS,
            vmem(Q_CHUNKS, 2, ROWS, WIDTH),
            vmem(2, 2, ROWS, LON),
            vmem(2, 2, ROWS, LON),
            vmem(*field),
            vmem(*field),
            vmem(*field),
            vmem(*field),
            vmem(2, LEV, 2, 6, ROWS, LON),
            dma((3, P_CHUNKS, 2)),
            dma((3, Q_CHUNKS, 2)),
            dma((2, 2, 2)),
            dma((2, 2, 2, 2)),
            dma((2, 2, 2, 2)),
            dma((2, 2, 2, 2)),
            dma((2, 2, 2)),
            dma((3,)),
            pltpu.SemaphoreType.REGULAR((2,)),
        ],
        compiler_params=pltpu.CompilerParams(
            collective_id=0, has_side_effects=True, vmem_limit_bytes=32 * 2**20
        ),
        name="ensemble_adjoint",
    )(ckpt_index, seeds, slot, current)
    return result.reshape(1, 3, LEV, ROWS, LON)


def solution(mesh):
    return jax.shard_map(
        on_device,
        mesh=mesh,
        in_specs=(
            P("member", None, None, "band", None),
            P(),
            P(None, None, None, "band", None),
            P("member"),
        ),
        out_specs=P("member", None, None, "band", None),
        check_vma=False,
    )
```

```python
import functools

import jax
import jax.numpy as jnp
from jax import lax
from jax.experimental import pallas as pl
from jax.experimental.pallas import tpu as pltpu
from jax.sharding import PartitionSpec as P

NY = 8
NZ = 6
NBAND = 16
CHIPS = NBAND // 2
LEV = 4
PLANES = 3 * LEV
HALF = PLANES // 2
ROWS = 8
LON = 512
LAST_SLOT = NY * NZ - 1
EDGE = {1: 4, 0: 2}
P_CHUNKS, Q_CHUNKS = HALF // 2, 4
WIDTH = LON // Q_CHUNKS
MESH = pl.DeviceIdType.MESH


def next_lon(x):
    return pltpu.roll(x, LON - 1, 1)


def prev_lon(x):
    return pltpu.roll(x, 1, 1)


def next_row(x):
    return pltpu.roll(x, 2 * ROWS - 1, 0)


def prev_row(x):
    return pltpu.roll(x, 1, 0)


def advance(east, north, height):
    diff_east = 0.1 * (next_lon(east) - prev_lon(east))
    diff_north = 0.1 * (next_lon(north) - prev_lon(north))
    diff_height = 0.1 * (next_lon(height) - prev_lon(height))
    return (
        east - (east * diff_east + diff_height),
        north - east * diff_north,
        height - (east * diff_height + diff_east),
    )


def coefficients(state):
    east, north, height = state
    depth = 0.1 * jnp.exp(0.25 * height)
    visc = 0.04 + 0.02 * jnp.tanh(height)
    east, north = 0.1 * east, 0.1 * north
    return depth, 1.0 - 4.0 * visc, visc + east, visc - east, visc + north, visc - north


def adjoint_step(factors, adjoint, keep):
    depth, middle, c_next, c_prev, r_next, r_prev = factors
    a, b, c = adjoint

    def spread(f, zonal=None, merid=None):
        if zonal is None:
            zonal = merid = 0.0
        return (
            middle * f
            + next_lon(c_next * f + zonal)
            + prev_lon(c_prev * f - zonal)
            + next_row(r_next * f + merid)
            + prev_row(r_prev * f - merid)
        )

    new_a = spread(a) + depth * (next_lon(c) - prev_lon(c))
    new_b = spread(b) + depth * (next_row(c) - prev_row(c))
    new_c = spread(c, 0.1 * a, 0.1 * b)
    return tuple(jnp.where(keep, f, 0.0) for f in (new_a, new_b, new_c))


def kernel(
    index_hbm, seed_ref, ckpt, innov, out,
    index_ref, slot,
    p_meter, p_rows_in, p_cols_in, p_last, p_mine, p_edge,
    q_meter, q_cols_in, q_rows_in, q_last, q_mine, q_edge,
    own, edge, force, force_edge, factor,
    p_sem, q_sem, gather_sem, cross_sem, spread_sem, edge_sem, force_sem, local_sem, ready_sem,
):
    band = lax.axis_index("band")
    member = lax.axis_index("member")
    y, z = lax.rem(member, NY), member // NY
    chip = band // 2
    odd = lax.rem(band, 2) == 1
    even = jnp.logical_not(odd)
    has_up, has_down = band < NBAND - 1, band > 0
    chip_up = chip < CHIPS - 1
    far_up, far_down = chip == CHIPS // 2 - 1, chip == CHIPS // 2
    near_up = jnp.logical_and(has_up, band != CHIPS - 1)
    near_down = jnp.logical_and(has_down, band != CHIPS)
    z_above = jnp.where(far_up, NZ - 1 - z, z)
    z_below = jnp.where(far_down, NZ - 1 - z, z)
    member_up = z_above * NY + y
    member_down = z_below * NY + y

    y_peers = [lax.rem(y + step, NY) for step in (4, 3, 5, 2, 6, 1, 7)]
    z_peers = [lax.rem(z + step, NZ) for step in range(1, NZ)]
    low_band, high_band = 2 * chip, 2 * chip + 1

    def at_y(peer, of_band):
        return {"band": of_band, "member": z * NY + peer}

    def at_z(peer, of_band):
        return {"band": of_band, "member": peer * NY + y}

    sibling = {"band": low_band + high_band - band}
    up = {"band": band + 1, "member": jnp.where(odd, member_up, member)}
    down = {"band": band - 1, "member": jnp.where(odd, member, member_down)}
    handler_up = {"band": band + 2, "member": member_up}
    handler_down = {"band": band - 2, "member": member_down}

    def low_rows(k):
        return slice(0, EDGE[k])

    def high_rows(k):
        return slice(ROWS - EDGE[k], ROWS)

    def p_part(peer, rows=slice(None)):
        planes = pl.ds((HALF // 2) * (peer // 4), HALF // 2)
        return planes, rows, pl.ds(pl.multiple_of(128 * lax.rem(peer, 4), 128), 128)

    def q_part(peer, rows=slice(None)):
        return HALF + peer, rows

    def p_chunk(peer, i):
        lanes = pl.ds(pl.multiple_of(128 * lax.rem(peer, 4), 128), 128)
        return P_CHUNKS * (peer // 4) + i, slice(None), lanes

    def q_lanes(i):
        return slice(WIDTH * i, WIDTH * (i + 1))

    def q_chunk(peer, i):
        return HALF + peer, slice(None), q_lanes(i)

    def send(src, dst, sems, device):
        return pltpu.make_async_remote_copy(
            src_ref=src, dst_ref=dst, send_sem=sems.at[0], recv_sem=sems.at[1],
            device_id=device, device_id_type=MESH,
        )

    def drain(ref, sems):
        return send(ref, ref, sems, sibling)

    def p_pieces(count, rows=slice(None)):
        return p_meter.at[:, pl.ds(0, count), rows]

    def q_planes(count, rows=slice(None)):
        return q_meter.at[:, pl.ds(0, count), rows]

    def copy(src, dst, number):
        return pltpu.make_async_copy(src, dst, local_sem.at[number])

    barrier = pltpu.get_barrier_semaphore()

    def greet(device):
        pl.semaphore_signal(barrier, inc=1, device_id=device, device_id_type=MESH)

    for peer in z_peers:
        greet(at_z(peer, high_band))
    for peer in y_peers:
        greet(at_y(peer, high_band))
    greet(sibling)

    @pl.when(odd)
    def _():
        for peer in z_peers:
            greet(at_z(peer, low_band))
        for peer in y_peers:
            greet(at_y(peer, low_band))
        pl.when(chip_up)(lambda: greet(up))
        pl.when(far_up)(lambda: greet(handler_up))

    pl.when(jnp.logical_and(even, near_down))(lambda: greet(down))

    load_slot = copy(ckpt, slot, 0)
    load_index = copy(index_hbm, index_ref, 1)
    load_force = copy(innov, force, 2)
    load_slot.start()
    load_index.start()
    load_force.start()
    load_slot.wait()
    peers = NY + NZ - 2
    alone = jnp.logical_or(far_up, chip == CHIPS - 1)
    plain = jnp.logical_not(jnp.logical_or(alone, far_down))
    for condition, count in (
        (band == 0, peers + 1),
        (jnp.logical_and(even, has_down), peers + 2),
        (jnp.logical_and(odd, alone), 2 * peers + 1),
        (jnp.logical_and(odd, plain), 2 * peers + 2),
        (jnp.logical_and(odd, far_down), 2 * peers + 3),
    ):
        pl.when(condition)(functools.partial(pl.semaphore_wait, barrier, count))

    def tell(number, device):
        pl.semaphore_signal(ready_sem.at[number], inc=1, device_id=device, device_id_type=MESH)

    pl.when(jnp.logical_and(even, far_down))(lambda: tell(0, down))
    pl.when(jnp.logical_and(odd, far_down))(lambda: tell(1, handler_down))

    def spots(core):
        return core * NZ + z, core * NY + y

    streams = [("q", 0), ("p", 0), ("q", 1), ("p", 1), ("q", 2), ("p", 2), ("q", 3)]

    def first_phase(core):
        q_spot, p_spot = spots(core)
        for kind, i in streams:
            if kind == "p":
                for peer in y_peers:
                    send(slot.at[p_chunk(peer, i)], p_rows_in[i].at[p_spot], p_sem.at[0, i], at_y(peer, high_band)).start()
                if core == 0:
                    send(slot.at[p_chunk(y, i)], p_rows_in[i].at[p_spot], p_sem.at[0, i], sibling).start()
                else:
                    p_rows_in[i][p_spot] = slot[p_chunk(y, i)]
            else:
                for peer in z_peers:
                    send(slot.at[q_chunk(peer, i)], q_cols_in[i].at[q_spot], q_sem.at[0, i], at_z(peer, high_band)).start()
                if core == 0:
                    send(slot.at[q_chunk(z, i)], q_cols_in[i].at[q_spot], q_sem.at[0, i], sibling).start()
                else:
                    q_cols_in[i][q_spot] = slot[q_chunk(z, i)]

    pl.when(even)(lambda: first_phase(0))
    pl.when(odd)(lambda: first_phase(1))

    everything, p_planes, q_planes_all = slice(0, PLANES), slice(0, HALF), slice(HALF, PLANES)

    def edge_up(src, dst, sems, k, planes, device):
        rows = (k, planes, high_rows(k))
        return send(src.at[rows], dst.at[rows], sems.at[k, 0], device)

    def edge_down(src, dst, sems, k, planes, device):
        rows = (k, planes, low_rows(k))
        return send(src.at[rows], dst.at[rows], sems.at[k, 1], device)

    def start_edges(src, dst, sems, k, planes, upward, downward):
        pl.when(upward)(lambda: edge_up(src, dst, sems, k, planes, up).start())
        pl.when(downward)(lambda: edge_down(src, dst, sems, k, planes, down).start())

    def finish_edges(src, dst, sems, k, planes, upward, downward):
        def upper():
            edge_up(src, dst, sems, k, planes, up).wait_send()
            edge_down(src, dst, sems, k, planes, up).wait_recv()

        def lower():
            edge_down(src, dst, sems, k, planes, down).wait_send()
            edge_up(src, dst, sems, k, planes, down).wait_recv()

        pl.when(upward)(upper)
        pl.when(downward)(lower)

    for k in (1, 0):
        start_edges(innov, force_edge, force_sem, k, everything, near_up, has_down)

    load_index.wait()
    seed = seed_ref[0]
    index = [index_ref[0], index_ref[1]]
    other = jnp.where(index[0] == LAST_SLOT, index[1], index[0])
    other_y, other_z = lax.rem(other, NY), other // NY
    load_force.wait()
    for k in range(2):
        for plane in range(PLANES):
            force[k, plane] = pltpu.roll(force[k, plane], seed, 1)

    @pl.when(odd)
    def _():
        for kind, i in streams:
            if kind == "p":
                drain(p_rows_in[i].at[pl.ds(0, 2 * NY - 1)], p_sem.at[0, i]).wait_recv()
                for core in range(2):
                    p_cols_in[i][z, core] = p_rows_in[i][core * NY + other_y]
                for peer in z_peers:
                    send(p_cols_in[i].at[z], p_cols_in[i].at[z], p_sem.at[1, i], at_z(peer, high_band)).start()

                @pl.when(z == NZ - 1)
                def _():
                    for core in range(2):
                        p_last[i, core] = p_rows_in[i][core * NY + NY - 1]
                    for peer in z_peers:
                        send(p_last.at[i], p_last.at[i], p_sem.at[2, i], at_z(peer, high_band)).start()
            else:
                drain(q_cols_in[i].at[pl.ds(0, 2 * NZ - 1)], q_sem.at[0, i]).wait_recv()
                for core in range(2):
                    q_rows_in[i][y, core] = q_cols_in[i][core * NZ + other_z]
                for peer in y_peers:
                    send(q_rows_in[i].at[y], q_rows_in[i].at[y], q_sem.at[1, i], at_y(peer, high_band)).start()

                @pl.when(y == NY - 1)
                def _():
                    for core in range(2):
                        q_last[i, core] = q_cols_in[i][core * NZ + NZ - 1]
                    for peer in y_peers:
                        send(q_last.at[i], q_last.at[i], q_sem.at[2, i], at_y(peer, high_band)).start()

        def cross_up(mine, landing, kind, k, rows):
            return send(
                mine.at[(k, 1) + rows(high_rows(k))], landing.at[(1, k) + rows(high_rows(k))],
                cross_sem.at[0, kind, k], handler_up,
            )

        def cross_down(mine, landing, kind, k, rows):
            return send(
                mine.at[(k, 0) + rows(low_rows(k))], landing.at[(0, k) + rows(low_rows(k))],
                cross_sem.at[1, kind, k], handler_down,
            )

        def p_rows(rows):
            return slice(None), rows

        def q_rows(rows):
            return (rows,)

        def start_cross(*job):
            pl.when(far_up)(lambda: cross_up(*job).start())
            pl.when(far_down)(lambda: cross_down(*job).start())

        for kind, i in streams:
            if kind == "p":
                drain(p_cols_in[i].at[pl.ds(0, NZ - 1)], p_sem.at[1, i]).wait()
                pl.when(z == NZ - 1)(lambda: drain(p_cols_in[i].at[pl.ds(0, NZ - 1)], p_sem.at[2, i]).wait_send())
                pl.when(z < NZ - 1)(lambda: drain(p_last.at[i], p_sem.at[2, i]).wait_recv())
                from_other, from_last = p_cols_in[i][other_z], p_last[i]
                for k in (1, 0):
                    p_mine[k, :, i] = jnp.where(index[k] == LAST_SLOT, from_last, from_other)
                place = (slice(None),) + p_chunk(y, i)
                send(p_mine.at[:, 0, i], own.at[place], gather_sem.at[0, 0], sibling).start()
                for peer in y_peers:
                    send(p_mine.at[:, 0, i], own.at[place], gather_sem.at[0, 0], at_y(peer, low_band)).start()
                    send(p_mine.at[:, 1, i], own.at[place], gather_sem.at[1, 0], at_y(peer, high_band)).start()
                if i == P_CHUNKS - 1:
                    @pl.when(far_up)
                    def _():
                        pl.semaphore_wait(ready_sem.at[0], 1)
                        pl.semaphore_wait(ready_sem.at[1], 1)
                        for k in (1, 0):
                            edge_up(innov, force_edge, force_sem, k, everything, up).start()

                for k in (1, 0):
                    own[(k,) + p_chunk(y, i)] = p_mine[k, 1, i]
                    if i == P_CHUNKS - 1:
                        start_cross(p_mine, p_edge, 0, k, p_rows)
            else:
                drain(q_rows_in[i].at[pl.ds(0, NY - 1)], q_sem.at[1, i]).wait()
                pl.when(y == NY - 1)(lambda: drain(q_rows_in[i].at[pl.ds(0, NY - 1)], q_sem.at[2, i]).wait_send())
                pl.when(y < NY - 1)(lambda: drain(q_last.at[i], q_sem.at[2, i]).wait_recv())
                from_other, from_last = q_rows_in[i][other_y], q_last[i]
                for k in (1, 0):
                    q_mine[k, :, :, q_lanes(i)] = jnp.where(index[k] == LAST_SLOT, from_last, from_other)
                place = (slice(None),) + q_chunk(z, i)
                send(q_mine.at[:, 0, :, q_lanes(i)], own.at[place], gather_sem.at[0, 1], sibling).start()
                for peer in z_peers:
                    send(q_mine.at[:, 0, :, q_lanes(i)], own.at[place], gather_sem.at[0, 1], at_z(peer, low_band)).start()
                    send(q_mine.at[:, 1, :, q_lanes(i)], own.at[place], gather_sem.at[1, 1], at_z(peer, high_band)).start()
                for k in (1, 0):
                    own[(k,) + q_chunk(z, i)] = q_mine[k, 1, :, q_lanes(i)]
                    if i == Q_CHUNKS - 1:
                        start_cross(q_mine, q_edge, 1, k, q_rows)

        def spread_p(k):
            @pl.when(far_down)
            def _():
                cross_up(p_mine, p_edge, 0, k, p_rows).wait_recv()
                piece, place = p_edge.at[1, k, :, high_rows(k)], (k,) + p_part(y, high_rows(k))
                send(piece, edge.at[place], spread_sem.at[0, k, 0], sibling).start()
                for peer in y_peers:
                    send(piece, edge.at[place], spread_sem.at[0, k, 0], at_y(peer, low_band)).start()

            @pl.when(far_up)
            def _():
                cross_down(p_mine, p_edge, 0, k, p_rows).wait_recv()
                piece, place = p_edge.at[0, k, :, low_rows(k)], (k,) + p_part(y, low_rows(k))
                for peer in y_peers:
                    send(piece, edge.at[place], spread_sem.at[1, k, 0], at_y(peer, high_band)).start()
                edge[place] = p_edge[0, k, :, low_rows(k)]

        def spread_q(k):
            @pl.when(far_down)
            def _():
                cross_up(q_mine, q_edge, 1, k, q_rows).wait_recv()
                piece, place = q_edge.at[1, k, high_rows(k)], (k,) + q_part(z_below, high_rows(k))
                send(piece, edge.at[place], spread_sem.at[0, k, 1], sibling).start()
                for peer in z_peers:
                    send(piece, edge.at[place], spread_sem.at[0, k, 1], at_z(peer, low_band)).start()

            @pl.when(far_up)
            def _():
                cross_down(q_mine, q_edge, 1, k, q_rows).wait_recv()
                piece, place = q_edge.at[0, k, low_rows(k)], (k,) + q_part(z_above, low_rows(k))
                for peer in z_peers:
                    send(piece, edge.at[place], spread_sem.at[1, k, 1], at_z(peer, high_band)).start()
                edge[place] = q_edge[0, k, low_rows(k)]

        for k in (1, 0):
            spread_p(k)
        for k in (1, 0):
            spread_q(k)

    def gathered(part, pieces, planes):
        pl.when(odd)(lambda: drain(pieces[0], gather_sem.at[1, part]).wait_recv())
        pl.when(even)(lambda: drain(pieces[1], gather_sem.at[0, part]).wait_recv())
        for k in (1, 0):
            start_edges(own, edge, edge_sem.at[part], k, planes, near_up, near_down)

    def factors_of(state):
        return coefficients(advance(*state)), coefficients(state)

    gathered(0, (p_pieces(2 * NY - 2), p_pieces(2 * NY)), p_planes)
    gathered(1, (q_planes(2 * NZ - 2), q_planes(2 * NZ)), q_planes_all)

    row = lax.broadcasted_iota(jnp.int32, (ROWS, LON), 0)
    inside = jnp.logical_not(
        jnp.logical_or(
            jnp.logical_and(band == NBAND - 1, row < ROWS // 2),
            jnp.logical_and(band == 0, row >= ROWS // 2),
        )
    )
    keep = jnp.logical_or(
        lax.broadcasted_iota(jnp.int32, (2 * ROWS, LON), 0) < ROWS,
        jnp.concatenate([inside, inside], axis=0),
    )

    for k in (1, 0):
        finish_edges(innov, force_edge, force_sem, k, everything, has_up, has_down)
        for plane in range(PLANES):
            force_edge[k, plane] = pltpu.roll(force_edge[k, plane], seed, 1)

    for k in (1, 0):
        for lev in range(LEV):
            state = tuple(own[k, comp * LEV + lev] for comp in range(3))
            for step, values in enumerate(factors_of(state)):
                for number, value in enumerate(values):
                    factor[k, lev, step, number] = value

    adjoint = [None] * LEV
    for k in (1, 0):
        @pl.when(jnp.logical_and(even, far_down))
        def _():
            drain(p_pieces(NY, high_rows(k)), spread_sem.at[0, k, 0]).wait_recv()
            drain(q_planes(NZ, high_rows(k)), spread_sem.at[0, k, 1]).wait_recv()

        @pl.when(jnp.logical_and(odd, far_up))
        def _():
            drain(p_pieces(NY - 1, low_rows(k)), spread_sem.at[1, k, 0]).wait_recv()
            drain(q_planes(NZ - 1, low_rows(k)), spread_sem.at[1, k, 1]).wait_recv()

        finish_edges(own, edge, edge_sem.at[0], k, p_planes, near_up, near_down)
        finish_edges(own, edge, edge_sem.at[1], k, q_planes_all, near_up, near_down)
        for lev in range(LEV):
            def both(inner_ref, outer_ref):
                return tuple(
                    jnp.concatenate(
                        [
                            inner_ref[k, comp * LEV + lev],
                            jnp.where(inside, outer_ref[k, comp * LEV + lev], 0.0),
                        ],
                        axis=0,
                    )
                    for comp in range(3)
                )

            forcing = both(force, force_edge)
            if adjoint[lev] is None:
                field = forcing
            else:
                field = tuple(f + g for f, g in zip(adjoint[lev], forcing))
            outer = tuple(jnp.where(inside, edge[k, comp * LEV + lev], 0.0) for comp in range(3))
            for step, values in enumerate(factors_of(outer)):
                whole = tuple(
                    jnp.concatenate([factor[k, lev, step, number], value], axis=0)
                    for number, value in enumerate(values)
                )
                field = adjoint_step(whole, field, keep)
            if k == 1:
                adjoint[lev] = field
            else:
                for comp in range(3):
                    out[comp * LEV + lev] = field[comp][:ROWS]

    def first_left(p_count, q_count):
        for i in range(P_CHUNKS):
            drain(p_rows_in[i].at[pl.ds(0, p_count)], p_sem.at[0, i]).wait_send()
        for i in range(Q_CHUNKS):
            drain(q_cols_in[i].at[pl.ds(0, q_count)], q_sem.at[0, i]).wait_send()

    pl.when(even)(lambda: first_left(NY, NZ))

    @pl.when(odd)
    def _():
        first_left(NY - 1, NZ - 1)
        drain(p_pieces(2 * NY), gather_sem.at[0, 0]).wait_send()
        drain(p_pieces(2 * NY - 2), gather_sem.at[1, 0]).wait_send()
        drain(q_planes(2 * NZ), gather_sem.at[0, 1]).wait_send()
        drain(q_planes(2 * NZ - 2), gather_sem.at[1, 1]).wait_send()
        for k in (1, 0):
            @pl.when(far_up)
            def _():
                drain(p_edge.at[0, k, :, high_rows(k)], cross_sem.at[0, 0, k]).wait_send()
                drain(q_edge.at[0, k, high_rows(k)], cross_sem.at[0, 1, k]).wait_send()
                drain(p_pieces(NY - 1, low_rows(k)), spread_sem.at[1, k, 0]).wait_send()
                drain(q_planes(NZ - 1, low_rows(k)), spread_sem.at[1, k, 1]).wait_send()

            @pl.when(far_down)
            def _():
                drain(p_edge.at[0, k, :, low_rows(k)], cross_sem.at[1, 0, k]).wait_send()
                drain(q_edge.at[0, k, low_rows(k)], cross_sem.at[1, 1, k]).wait_send()
                drain(p_pieces(NY, high_rows(k)), spread_sem.at[0, k, 0]).wait_send()
                drain(q_planes(NZ, high_rows(k)), spread_sem.at[0, k, 1]).wait_send()


def on_device(checkpoints, ckpt_index, innovations, seeds):
    slot = checkpoints.reshape(PLANES, ROWS, LON)
    current = innovations.reshape(2, PLANES, ROWS, LON)
    hbm = pl.BlockSpec(memory_space=pltpu.HBM)
    slot, current, ckpt_index = (
        pltpu.with_memory_space_constraint(operand, pltpu.HBM) for operand in (slot, current, ckpt_index)
    )
    field = (2, PLANES, ROWS, LON)
    dma = pltpu.SemaphoreType.DMA

    def vmem(*shape):
        return pltpu.VMEM(shape, jnp.float32)

    result = pl.pallas_call(
        kernel,
        out_shape=jax.ShapeDtypeStruct((PLANES, ROWS, LON), jnp.float32),
        in_specs=[hbm, pl.BlockSpec(memory_space=pltpu.SMEM), hbm, hbm],
        out_specs=pl.BlockSpec(memory_space=pltpu.VMEM),
        scratch_shapes=[
            pltpu.SMEM((2,), jnp.int32),
            vmem(PLANES, ROWS, LON),
            vmem(P_CHUNKS, 2 * NY, ROWS, 128),
            [vmem(2 * NY, ROWS, 128)] * P_CHUNKS,
            [vmem(NZ, 2, ROWS, 128)] * P_CHUNKS,
            vmem(P_CHUNKS, 2, ROWS, 128),
            vmem(2, 2, P_CHUNKS, ROWS, 128),
            vmem(2, 2, P_CHUNKS, ROWS, 128),
            vmem(Q_CHUNKS, 2 * NZ, ROWS, WIDTH),
            [vmem(2 * NZ, ROWS, WIDTH)] * Q_CHUNKS,
            [vmem(NY, 2, ROWS, WIDTH)] * Q_CHUNKS,
            vmem(Q_CHUNKS, 2, ROWS, WIDTH),
            vmem(2, 2, ROWS, LON),
            vmem(2, 2, ROWS, LON),
            vmem(*field),
            vmem(*field),
            vmem(*field),
            vmem(*field),
            vmem(2, LEV, 2, 6, ROWS, LON),
            dma((3, P_CHUNKS, 2)),
            dma((3, Q_CHUNKS, 2)),
            dma((2, 2, 2)),
            dma((2, 2, 2, 2)),
            dma((2, 2, 2, 2)),
            dma((2, 2, 2, 2)),
            dma((2, 2, 2)),
            dma((3,)),
            pltpu.SemaphoreType.REGULAR((2,)),
        ],
        compiler_params=pltpu.CompilerParams(
            collective_id=0, has_side_effects=True, vmem_limit_bytes=32 * 2**20
        ),
        name="ensemble_adjoint",
    )(ckpt_index, seeds, slot, current)
    return result.reshape(1, 3, LEV, ROWS, LON)


def solution(mesh):
    return jax.shard_map(
        on_device,
        mesh=mesh,
        in_specs=(
            P("member", None, None, "band", None),
            P(),
            P(None, None, None, "band", None),
            P("member"),
        ),
        out_specs=P("member", None, None, "band", None),
        check_vma=False,
    )
```

```python
import functools

import jax
import jax.numpy as jnp
from jax import lax
from jax.experimental import pallas as pl
from jax.experimental.pallas import tpu as pltpu
from jax.sharding import PartitionSpec as P

NY = 8
NZ = 6
NBAND = 16
CHIPS = NBAND // 2
LEV = 4
PLANES = 3 * LEV
HALF = PLANES // 2
ROWS = 8
LON = 512
LAST_SLOT = NY * NZ - 1
EDGE = {1: 4, 0: 2}
P_CHUNKS, Q_CHUNKS = HALF // 2, 4
WIDTH = LON // Q_CHUNKS
MESH = pl.DeviceIdType.MESH


def next_lon(x):
    return pltpu.roll(x, LON - 1, 1)


def prev_lon(x):
    return pltpu.roll(x, 1, 1)


def next_row(x):
    return pltpu.roll(x, 2 * ROWS - 1, 0)


def prev_row(x):
    return pltpu.roll(x, 1, 0)


def advance(east, north, height):
    diff_east = 0.1 * (next_lon(east) - prev_lon(east))
    diff_north = 0.1 * (next_lon(north) - prev_lon(north))
    diff_height = 0.1 * (next_lon(height) - prev_lon(height))
    return (
        east - (east * diff_east + diff_height),
        north - east * diff_north,
        height - (east * diff_height + diff_east),
    )


def coefficients(state):
    east, north, height = state
    depth = 0.1 * jnp.exp(0.25 * height)
    visc = 0.04 + 0.02 * jnp.tanh(height)
    east, north = 0.1 * east, 0.1 * north
    return depth, 1.0 - 4.0 * visc, visc + east, visc - east, visc + north, visc - north


def adjoint_step(factors, adjoint, keep):
    depth, middle, c_next, c_prev, r_next, r_prev = factors
    a, b, c = adjoint

    def spread(f, zonal=None, merid=None):
        if zonal is None:
            zonal = merid = 0.0
        return (
            middle * f
            + next_lon(c_next * f + zonal)
            + prev_lon(c_prev * f - zonal)
            + next_row(r_next * f + merid)
            + prev_row(r_prev * f - merid)
        )

    new_a = spread(a) + depth * (next_lon(c) - prev_lon(c))
    new_b = spread(b) + depth * (next_row(c) - prev_row(c))
    new_c = spread(c, 0.1 * a, 0.1 * b)
    return tuple(jnp.where(keep, f, 0.0) for f in (new_a, new_b, new_c))


def kernel(
    index_hbm, seed_ref, ckpt, innov, out,
    index_ref, slot,
    p_meter, p_rows_in, p_cols_in, p_last, p_mine, p_edge,
    q_meter, q_cols_in, q_rows_in, q_last, q_mine, q_edge,
    own, edge, force, force_edge, factor,
    p_sem, q_sem, gather_sem, cross_sem, spread_sem, edge_sem, force_sem, local_sem, ready_sem,
):
    band = lax.axis_index("band")
    member = lax.axis_index("member")
    y, z = lax.rem(member, NY), member // NY
    chip = band // 2
    odd = lax.rem(band, 2) == 1
    even = jnp.logical_not(odd)
    has_up, has_down = band < NBAND - 1, band > 0
    chip_up = chip < CHIPS - 1
    far_up, far_down = chip == CHIPS // 2 - 1, chip == CHIPS // 2
    near_up = jnp.logical_and(has_up, band != CHIPS - 1)
    near_down = jnp.logical_and(has_down, band != CHIPS)
    z_above = jnp.where(far_up, NZ - 1 - z, z)
    z_below = jnp.where(far_down, NZ - 1 - z, z)
    member_up = z_above * NY + y
    member_down = z_below * NY + y

    y_peers = [lax.rem(y + step, NY) for step in (4, 3, 5, 2, 6, 1, 7)]
    z_peers = [lax.rem(z + jnp.where(z < NZ // 2, NZ - step, step), NZ) for step in range(1, NZ)]
    low_band, high_band = 2 * chip, 2 * chip + 1

    def at_y(peer, of_band):
        return {"band": of_band, "member": z * NY + peer}

    def at_z(peer, of_band):
        return {"band": of_band, "member": peer * NY + y}

    sibling = {"band": low_band + high_band - band}
    up = {"band": band + 1, "member": jnp.where(odd, member_up, member)}
    down = {"band": band - 1, "member": jnp.where(odd, member, member_down)}
    handler_up = {"band": band + 2, "member": member_up}
    handler_down = {"band": band - 2, "member": member_down}

    def low_rows(k):
        return slice(0, EDGE[k])

    def high_rows(k):
        return slice(ROWS - EDGE[k], ROWS)

    def p_part(peer, rows=slice(None)):
        planes = pl.ds((HALF // 2) * (peer // 4), HALF // 2)
        return planes, rows, pl.ds(pl.multiple_of(128 * lax.rem(peer, 4), 128), 128)

    def q_part(peer, rows=slice(None)):
        return HALF + peer, rows

    def p_chunk(peer, i):
        lanes = pl.ds(pl.multiple_of(128 * lax.rem(peer, 4), 128), 128)
        return P_CHUNKS * (peer // 4) + i, slice(None), lanes

    def q_lanes(i):
        return slice(WIDTH * i, WIDTH * (i + 1))

    def q_chunk(peer, i):
        return HALF + peer, slice(None), q_lanes(i)

    def send(src, dst, sems, device):
        return pltpu.make_async_remote_copy(
            src_ref=src, dst_ref=dst, send_sem=sems.at[0], recv_sem=sems.at[1],
            device_id=device, device_id_type=MESH,
        )

    def drain(ref, sems):
        return send(ref, ref, sems, sibling)

    def p_pieces(count, rows=slice(None)):
        return p_meter.at[:, pl.ds(0, count), rows]

    def q_planes(count, rows=slice(None)):
        return q_meter.at[:, pl.ds(0, count), rows]

    def copy(src, dst, number):
        return pltpu.make_async_copy(src, dst, local_sem.at[number])

    barrier = pltpu.get_barrier_semaphore()

    def greet(device):
        pl.semaphore_signal(barrier, inc=1, device_id=device, device_id_type=MESH)

    for peer in z_peers:
        greet(at_z(peer, high_band))
    for peer in y_peers:
        greet(at_y(peer, high_band))
    greet(sibling)

    @pl.when(odd)
    def _():
        for peer in z_peers:
            greet(at_z(peer, low_band))
        for peer in y_peers:
            greet(at_y(peer, low_band))
        pl.when(chip_up)(lambda: greet(up))
        pl.when(far_up)(lambda: greet(handler_up))

    pl.when(jnp.logical_and(even, near_down))(lambda: greet(down))

    load_slot = copy(ckpt, slot, 0)
    load_index = copy(index_hbm, index_ref, 1)
    load_force = copy(innov, force, 2)
    load_slot.start()
    load_index.start()
    load_force.start()
    load_slot.wait()
    peers = NY + NZ - 2
    alone = jnp.logical_or(far_up, chip == CHIPS - 1)
    plain = jnp.logical_not(jnp.logical_or(alone, far_down))
    for condition, count in (
        (band == 0, peers + 1),
        (jnp.logical_and(even, has_down), peers + 2),
        (jnp.logical_and(odd, alone), 2 * peers + 1),
        (jnp.logical_and(odd, plain), 2 * peers + 2),
        (jnp.logical_and(odd, far_down), 2 * peers + 3),
    ):
        pl.when(condition)(functools.partial(pl.semaphore_wait, barrier, count))

    def tell(number, device):
        pl.semaphore_signal(ready_sem.at[number], inc=1, device_id=device, device_id_type=MESH)

    pl.when(jnp.logical_and(even, far_down))(lambda: tell(0, down))
    pl.when(jnp.logical_and(odd, far_down))(lambda: tell(1, handler_down))

    def spots(core):
        return core * NZ + z, core * NY + y

    streams = [("q", 0), ("p", 0), ("q", 1), ("p", 1), ("q", 2), ("p", 2), ("q", 3)]

    def first_phase(core):
        q_spot, p_spot = spots(core)
        for kind, i in streams:
            if kind == "p":
                for peer in y_peers:
                    send(slot.at[p_chunk(peer, i)], p_rows_in[i].at[p_spot], p_sem.at[0, i], at_y(peer, high_band)).start()
                if core == 0:
                    send(slot.at[p_chunk(y, i)], p_rows_in[i].at[p_spot], p_sem.at[0, i], sibling).start()
                else:
                    p_rows_in[i][p_spot] = slot[p_chunk(y, i)]
            else:
                for peer in z_peers:
                    send(slot.at[q_chunk(peer, i)], q_cols_in[i].at[q_spot], q_sem.at[0, i], at_z(peer, high_band)).start()
                if core == 0:
                    send(slot.at[q_chunk(z, i)], q_cols_in[i].at[q_spot], q_sem.at[0, i], sibling).start()
                else:
                    q_cols_in[i][q_spot] = slot[q_chunk(z, i)]

    pl.when(even)(lambda: first_phase(0))
    pl.when(odd)(lambda: first_phase(1))

    everything, p_planes, q_planes_all = slice(0, PLANES), slice(0, HALF), slice(HALF, PLANES)

    def edge_up(src, dst, sems, k, planes, device):
        rows = (k, planes, high_rows(k))
        return send(src.at[rows], dst.at[rows], sems.at[k, 0], device)

    def edge_down(src, dst, sems, k, planes, device):
        rows = (k, planes, low_rows(k))
        return send(src.at[rows], dst.at[rows], sems.at[k, 1], device)

    def start_edges(src, dst, sems, k, planes, upward, downward):
        pl.when(upward)(lambda: edge_up(src, dst, sems, k, planes, up).start())
        pl.when(downward)(lambda: edge_down(src, dst, sems, k, planes, down).start())

    def finish_edges(src, dst, sems, k, planes, upward, downward):
        def upper():
            edge_up(src, dst, sems, k, planes, up).wait_send()
            edge_down(src, dst, sems, k, planes, up).wait_recv()

        def lower():
            edge_down(src, dst, sems, k, planes, down).wait_send()
            edge_up(src, dst, sems, k, planes, down).wait_recv()

        pl.when(upward)(upper)
        pl.when(downward)(lower)

    for k in (1, 0):
        start_edges(innov, force_edge, force_sem, k, everything, near_up, has_down)

    load_index.wait()
    seed = seed_ref[0]
    index = [index_ref[0], index_ref[1]]
    other = jnp.where(index[0] == LAST_SLOT, index[1], index[0])
    other_y, other_z = lax.rem(other, NY), other // NY
    load_force.wait()
    for k in range(2):
        for plane in range(PLANES):
            force[k, plane] = pltpu.roll(force[k, plane], seed, 1)

    @pl.when(odd)
    def _():
        for kind, i in streams:
            if kind == "p":
                drain(p_rows_in[i].at[pl.ds(0, 2 * NY - 1)], p_sem.at[0, i]).wait_recv()
                for core in range(2):
                    p_cols_in[i][z, core] = p_rows_in[i][core * NY + other_y]
                for peer in z_peers:
                    send(p_cols_in[i].at[z], p_cols_in[i].at[z], p_sem.at[1, i], at_z(peer, high_band)).start()

                @pl.when(z == NZ - 1)
                def _():
                    for core in range(2):
                        p_last[i, core] = p_rows_in[i][core * NY + NY - 1]
                    for peer in z_peers:
                        send(p_last.at[i], p_last.at[i], p_sem.at[2, i], at_z(peer, high_band)).start()
            else:
                drain(q_cols_in[i].at[pl.ds(0, 2 * NZ - 1)], q_sem.at[0, i]).wait_recv()
                for core in range(2):
                    q_rows_in[i][y, core] = q_cols_in[i][core * NZ + other_z]
                for peer in y_peers:
                    send(q_rows_in[i].at[y], q_rows_in[i].at[y], q_sem.at[1, i], at_y(peer, high_band)).start()

                @pl.when(y == NY - 1)
                def _():
                    for core in range(2):
                        q_last[i, core] = q_cols_in[i][core * NZ + NZ - 1]
                    for peer in y_peers:
                        send(q_last.at[i], q_last.at[i], q_sem.at[2, i], at_y(peer, high_band)).start()

        def cross_up(mine, landing, kind, k, rows):
            return send(
                mine.at[(k, 1) + rows(high_rows(k))], landing.at[(1, k) + rows(high_rows(k))],
                cross_sem.at[0, kind, k], handler_up,
            )

        def cross_down(mine, landing, kind, k, rows):
            return send(
                mine.at[(k, 0) + rows(low_rows(k))], landing.at[(0, k) + rows(low_rows(k))],
                cross_sem.at[1, kind, k], handler_down,
            )

        def p_rows(rows):
            return slice(None), rows

        def q_rows(rows):
            return (rows,)

        def start_cross(*job):
            pl.when(far_up)(lambda: cross_up(*job).start())
            pl.when(far_down)(lambda: cross_down(*job).start())

        for kind, i in streams:
            if kind == "p":
                drain(p_cols_in[i].at[pl.ds(0, NZ - 1)], p_sem.at[1, i]).wait()
                pl.when(z == NZ - 1)(lambda: drain(p_cols_in[i].at[pl.ds(0, NZ - 1)], p_sem.at[2, i]).wait_send())
                pl.when(z < NZ - 1)(lambda: drain(p_last.at[i], p_sem.at[2, i]).wait_recv())
                from_other, from_last = p_cols_in[i][other_z], p_last[i]
                for k in (1, 0):
                    p_mine[k, :, i] = jnp.where(index[k] == LAST_SLOT, from_last, from_other)
                if i == P_CHUNKS - 1:
                    @pl.when(far_up)
                    def _():
                        pl.semaphore_wait(ready_sem.at[0], 1)
                        pl.semaphore_wait(ready_sem.at[1], 1)
                        for k in (1, 0):
                            edge_up(innov, force_edge, force_sem, k, everything, up).start()
                if i == P_CHUNKS - 1:
                    for k in (1, 0):
                        start_cross(p_mine, p_edge, 0, k, p_rows)
                place = (slice(None),) + p_chunk(y, i)
                send(p_mine.at[:, 0, i], own.at[place], gather_sem.at[0, 0], sibling).start()
                for peer in y_peers:
                    send(p_mine.at[:, 0, i], own.at[place], gather_sem.at[0, 0], at_y(peer, low_band)).start()
                    send(p_mine.at[:, 1, i], own.at[place], gather_sem.at[1, 0], at_y(peer, high_band)).start()
                for k in (1, 0):
                    own[(k,) + p_chunk(y, i)] = p_mine[k, 1, i]
            else:
                drain(q_rows_in[i].at[pl.ds(0, NY - 1)], q_sem.at[1, i]).wait()
                pl.when(y == NY - 1)(lambda: drain(q_rows_in[i].at[pl.ds(0, NY - 1)], q_sem.at[2, i]).wait_send())
                pl.when(y < NY - 1)(lambda: drain(q_last.at[i], q_sem.at[2, i]).wait_recv())
                from_other, from_last = q_rows_in[i][other_y], q_last[i]
                for k in (1, 0):
                    q_mine[k, :, :, q_lanes(i)] = jnp.where(index[k] == LAST_SLOT, from_last, from_other)
                if i == Q_CHUNKS - 1:
                    for k in (1, 0):
                        start_cross(q_mine, q_edge, 1, k, q_rows)
                place = (slice(None),) + q_chunk(z, i)
                send(q_mine.at[:, 0, :, q_lanes(i)], own.at[place], gather_sem.at[0, 1], sibling).start()
                for peer in z_peers:
                    send(q_mine.at[:, 0, :, q_lanes(i)], own.at[place], gather_sem.at[0, 1], at_z(peer, low_band)).start()
                    send(q_mine.at[:, 1, :, q_lanes(i)], own.at[place], gather_sem.at[1, 1], at_z(peer, high_band)).start()
                for k in (1, 0):
                    own[(k,) + q_chunk(z, i)] = q_mine[k, 1, :, q_lanes(i)]

        def spread_p(k):
            @pl.when(far_down)
            def _():
                cross_up(p_mine, p_edge, 0, k, p_rows).wait_recv()
                piece, place = p_edge.at[1, k, :, high_rows(k)], (k,) + p_part(y, high_rows(k))
                send(piece, edge.at[place], spread_sem.at[0, k, 0], sibling).start()
                for peer in y_peers:
                    send(piece, edge.at[place], spread_sem.at[0, k, 0], at_y(peer, low_band)).start()

            @pl.when(far_up)
            def _():
                cross_down(p_mine, p_edge, 0, k, p_rows).wait_recv()
                piece, place = p_edge.at[0, k, :, low_rows(k)], (k,) + p_part(y, low_rows(k))
                for peer in y_peers:
                    send(piece, edge.at[place], spread_sem.at[1, k, 0], at_y(peer, high_band)).start()
                edge[place] = p_edge[0, k, :, low_rows(k)]

        def spread_q(k):
            @pl.when(far_down)
            def _():
                cross_up(q_mine, q_edge, 1, k, q_rows).wait_recv()
                piece, place = q_edge.at[1, k, high_rows(k)], (k,) + q_part(z_below, high_rows(k))
                send(piece, edge.at[place], spread_sem.at[0, k, 1], sibling).start()
                for peer in z_peers:
                    send(piece, edge.at[place], spread_sem.at[0, k, 1], at_z(peer, low_band)).start()

            @pl.when(far_up)
            def _():
                cross_down(q_mine, q_edge, 1, k, q_rows).wait_recv()
                piece, place = q_edge.at[0, k, low_rows(k)], (k,) + q_part(z_above, low_rows(k))
                for peer in z_peers:
                    send(piece, edge.at[place], spread_sem.at[1, k, 1], at_z(peer, high_band)).start()
                edge[place] = q_edge[0, k, low_rows(k)]

        for k in (1, 0):
            spread_p(k)
        for k in (1, 0):
            spread_q(k)

    def gathered(part, pieces, planes):
        pl.when(odd)(lambda: drain(pieces[0], gather_sem.at[1, part]).wait_recv())
        pl.when(even)(lambda: drain(pieces[1], gather_sem.at[0, part]).wait_recv())
        for k in (1, 0):
            start_edges(own, edge, edge_sem.at[part], k, planes, near_up, near_down)

    def factors_of(state):
        return coefficients(advance(*state)), coefficients(state)

    gathered(0, (p_pieces(2 * NY - 2), p_pieces(2 * NY)), p_planes)
    gathered(1, (q_planes(2 * NZ - 2), q_planes(2 * NZ)), q_planes_all)

    row = lax.broadcasted_iota(jnp.int32, (ROWS, LON), 0)
    inside = jnp.logical_not(
        jnp.logical_or(
            jnp.logical_and(band == NBAND - 1, row < ROWS // 2),
            jnp.logical_and(band == 0, row >= ROWS // 2),
        )
    )
    keep = jnp.logical_or(
        lax.broadcasted_iota(jnp.int32, (2 * ROWS, LON), 0) < ROWS,
        jnp.concatenate([inside, inside], axis=0),
    )

    for k in (1, 0):
        finish_edges(innov, force_edge, force_sem, k, everything, has_up, has_down)
        for plane in range(PLANES):
            force_edge[k, plane] = pltpu.roll(force_edge[k, plane], seed, 1)

    for k in (1, 0):
        for lev in range(LEV):
            state = tuple(own[k, comp * LEV + lev] for comp in range(3))
            for step, values in enumerate(factors_of(state)):
                for number, value in enumerate(values):
                    factor[k, lev, step, number] = value

    adjoint = [None] * LEV
    for k in (1, 0):
        @pl.when(jnp.logical_and(even, far_down))
        def _():
            drain(p_pieces(NY, high_rows(k)), spread_sem.at[0, k, 0]).wait_recv()
            drain(q_planes(NZ, high_rows(k)), spread_sem.at[0, k, 1]).wait_recv()

        @pl.when(jnp.logical_and(odd, far_up))
        def _():
            drain(p_pieces(NY - 1, low_rows(k)), spread_sem.at[1, k, 0]).wait_recv()
            drain(q_planes(NZ - 1, low_rows(k)), spread_sem.at[1, k, 1]).wait_recv()

        finish_edges(own, edge, edge_sem.at[0], k, p_planes, near_up, near_down)
        finish_edges(own, edge, edge_sem.at[1], k, q_planes_all, near_up, near_down)
        for lev in range(LEV):
            def both(inner_ref, outer_ref):
                return tuple(
                    jnp.concatenate(
                        [
                            inner_ref[k, comp * LEV + lev],
                            jnp.where(inside, outer_ref[k, comp * LEV + lev], 0.0),
                        ],
                        axis=0,
                    )
                    for comp in range(3)
                )

            forcing = both(force, force_edge)
            if adjoint[lev] is None:
                field = forcing
            else:
                field = tuple(f + g for f, g in zip(adjoint[lev], forcing))
            outer = tuple(jnp.where(inside, edge[k, comp * LEV + lev], 0.0) for comp in range(3))
            for step, values in enumerate(factors_of(outer)):
                whole = tuple(
                    jnp.concatenate([factor[k, lev, step, number], value], axis=0)
                    for number, value in enumerate(values)
                )
                field = adjoint_step(whole, field, keep)
            if k == 1:
                adjoint[lev] = field
            else:
                for comp in range(3):
                    out[comp * LEV + lev] = field[comp][:ROWS]

    def first_left(p_count, q_count):
        for i in range(P_CHUNKS):
            drain(p_rows_in[i].at[pl.ds(0, p_count)], p_sem.at[0, i]).wait_send()
        for i in range(Q_CHUNKS):
            drain(q_cols_in[i].at[pl.ds(0, q_count)], q_sem.at[0, i]).wait_send()

    pl.when(even)(lambda: first_left(NY, NZ))

    @pl.when(odd)
    def _():
        first_left(NY - 1, NZ - 1)
        drain(p_pieces(2 * NY), gather_sem.at[0, 0]).wait_send()
        drain(p_pieces(2 * NY - 2), gather_sem.at[1, 0]).wait_send()
        drain(q_planes(2 * NZ), gather_sem.at[0, 1]).wait_send()
        drain(q_planes(2 * NZ - 2), gather_sem.at[1, 1]).wait_send()
        for k in (1, 0):
            @pl.when(far_up)
            def _():
                drain(p_edge.at[0, k, :, high_rows(k)], cross_sem.at[0, 0, k]).wait_send()
                drain(q_edge.at[0, k, high_rows(k)], cross_sem.at[0, 1, k]).wait_send()
                drain(p_pieces(NY - 1, low_rows(k)), spread_sem.at[1, k, 0]).wait_send()
                drain(q_planes(NZ - 1, low_rows(k)), spread_sem.at[1, k, 1]).wait_send()

            @pl.when(far_down)
            def _():
                drain(p_edge.at[0, k, :, low_rows(k)], cross_sem.at[1, 0, k]).wait_send()
                drain(q_edge.at[0, k, low_rows(k)], cross_sem.at[1, 1, k]).wait_send()
                drain(p_pieces(NY, high_rows(k)), spread_sem.at[0, k, 0]).wait_send()
                drain(q_planes(NZ, high_rows(k)), spread_sem.at[0, k, 1]).wait_send()


def on_device(checkpoints, ckpt_index, innovations, seeds):
    slot = checkpoints.reshape(PLANES, ROWS, LON)
    current = innovations.reshape(2, PLANES, ROWS, LON)
    hbm = pl.BlockSpec(memory_space=pltpu.HBM)
    slot, current, ckpt_index = (
        pltpu.with_memory_space_constraint(operand, pltpu.HBM) for operand in (slot, current, ckpt_index)
    )
    field = (2, PLANES, ROWS, LON)
    dma = pltpu.SemaphoreType.DMA

    def vmem(*shape):
        return pltpu.VMEM(shape, jnp.float32)

    result = pl.pallas_call(
        kernel,
        out_shape=jax.ShapeDtypeStruct((PLANES, ROWS, LON), jnp.float32),
        in_specs=[hbm, pl.BlockSpec(memory_space=pltpu.SMEM), hbm, hbm],
        out_specs=pl.BlockSpec(memory_space=pltpu.VMEM),
        scratch_shapes=[
            pltpu.SMEM((2,), jnp.int32),
            vmem(PLANES, ROWS, LON),
            vmem(P_CHUNKS, 2 * NY, ROWS, 128),
            [vmem(2 * NY, ROWS, 128)] * P_CHUNKS,
            [vmem(NZ, 2, ROWS, 128)] * P_CHUNKS,
            vmem(P_CHUNKS, 2, ROWS, 128),
            vmem(2, 2, P_CHUNKS, ROWS, 128),
            vmem(2, 2, P_CHUNKS, ROWS, 128),
            vmem(Q_CHUNKS, 2 * NZ, ROWS, WIDTH),
            [vmem(2 * NZ, ROWS, WIDTH)] * Q_CHUNKS,
            [vmem(NY, 2, ROWS, WIDTH)] * Q_CHUNKS,
            vmem(Q_CHUNKS, 2, ROWS, WIDTH),
            vmem(2, 2, ROWS, LON),
            vmem(2, 2, ROWS, LON),
            vmem(*field),
            vmem(*field),
            vmem(*field),
            vmem(*field),
            vmem(2, LEV, 2, 6, ROWS, LON),
            dma((3, P_CHUNKS, 2)),
            dma((3, Q_CHUNKS, 2)),
            dma((2, 2, 2)),
            dma((2, 2, 2, 2)),
            dma((2, 2, 2, 2)),
            dma((2, 2, 2, 2)),
            dma((2, 2, 2)),
            dma((3,)),
            pltpu.SemaphoreType.REGULAR((2,)),
        ],
        compiler_params=pltpu.CompilerParams(
            collective_id=0, has_side_effects=True, vmem_limit_bytes=32 * 2**20
        ),
        name="ensemble_adjoint",
    )(ckpt_index, seeds, slot, current)
    return result.reshape(1, 3, LEV, ROWS, LON)


def solution(mesh):
    return jax.shard_map(
        on_device,
        mesh=mesh,
        in_specs=(
            P("member", None, None, "band", None),
            P(),
            P(None, None, None, "band", None),
            P("member"),
        ),
        out_specs=P("member", None, None, "band", None),
        check_vma=False,
    )
```
